256 devices in a mesh: frames: 8 (over y, x_lo), height: 32 (over x_hi, z, core).
Axes of the slice: x: 4 (x_hi: 2, x_lo: 2; x = x_hi * 2 + x_lo), y: 4, z: 8, core: 2. Of those that a mesh axis runs over, the one named last changes fastest.
Arguments:
- latent: bfloat16 [8, 64, 160, 384], P('frames', 'height'), may hold values from -15 to 15
- first_gain: float32 [384], replicated, may hold values from 0.1 to 1.9
- first_shift: float32 [384], replicated, may hold values from -4 to 4
- query_weight: bfloat16 [384, 384], replicated
- key_weight: bfloat16 [384, 384], replicated
- value_weight: bfloat16 [384, 384], replicated, may hold values from -0.3125 to 0.3125
- out_weight: bfloat16 [384, 384], replicated, may hold values from -0.3125 to 0.3125
- out_bias: float32 [384], replicated, may hold values from -6 to 6
- second_gain: float32 [384], replicated, may hold values from 0.1 to 1.9
- second_shift: float32 [384], replicated, may hold values from -4 to 4
- up_weight: bfloat16 [3, 3, 3, 384, 384], replicated, may hold values from -0.15625 to 0.15625
- up_bias: float32 [384], replicated, may hold values from -6 to 6
Outputs:
- upsampled: bfloat16 [16, 128, 320, 384], P('frames', 'height')
The draws below stay inside these ranges and needn't reach their ends.
All inputs are finite; a program needn't handle non-finite values.
Results may differ from the reference program's by a relative error of at most 0.013.
Values may be sent and summed in bfloat16 or wider, within the bound.
A program may use at most 128 MiB of HBM per device.

```python
import math
import jax
import jax.numpy as jnp
from jax import lax

C = 384
GROUPS = 32
WID = 160
ROWS_DEV = 2
F = 8
H = 64


def draw_latent(key, part):
    keys = jax.random.split(jax.random.fold_in(key, 11), 8)
    frame_pos = jnp.arange(F, dtype=jnp.float32)[:, None, None, None]
    row_index = jnp.arange(H, dtype=jnp.int32)
    row_pos = row_index.astype(jnp.float32)[None, :, None, None]
    ramp = 0.5 * (frame_pos / max(F - 1, 1) + row_pos / max(H - 1, 1))
    rough = jnp.exp(jax.random.uniform(keys[0], (F, H, WID, 1), jnp.float32, 0.0, math.log(3.3)))
    position_scale = jnp.exp(math.log(3.0) * ramp) * rough
    channel_scale = jnp.exp(jax.random.uniform(keys[1], (C,), jnp.float32, 0.0, math.log(10.0)))
    offsets = jax.random.normal(keys[2], (H // ROWS_DEV, C), jnp.float32)
    slab_offset = offsets[row_index // ROWS_DEV][None, :, None, :]
    frame_offset = 1.1 * jax.random.normal(keys[7], (F, 1, 1, C), jnp.float32)
    base = jax.random.normal(keys[3], (F, H, WID, C), jnp.float32)
    result = 0.3 * channel_scale * (position_scale * base + slab_offset + frame_offset)
    return (0.25 * jnp.clip(result, -60.0, 60.0)).astype(jnp.bfloat16)


def weight_pair(key):
    first_key, second_key = jax.random.split(jax.random.fold_in(key, 29))
    bound = 4.0 / math.sqrt(C)
    first = jax.random.normal(first_key, (C, C), jnp.float32) / math.sqrt(C)
    other = jax.random.normal(second_key, (C, C), jnp.float32) / math.sqrt(C)
    second = other
    return (jnp.clip(first, -bound, bound), jnp.clip(second, -bound, bound))


def draw_query_weight(key, part):
    return weight_pair(key)[0].astype(jnp.bfloat16)


def draw_key_weight(key, part):
    return weight_pair(key)[1].astype(jnp.bfloat16)


def normal_values(key, shape, scale, limit, held_as=jnp.bfloat16):
    drawn = scale * jax.random.normal(key, shape, jnp.float32)
    return jnp.clip(drawn, min=-limit, max=limit).astype(held_as)


def setup_inputs(seed: int = 0) -> dict:
    arg_keys = jax.random.split(jax.random.key(seed), 13)
    latent = draw_latent(jax.random.fold_in(arg_keys[12], 71), 0)
    first_gain = jnp.clip(1.0 + 0.18 * jax.random.normal(arg_keys[1], (C,), jnp.float32), 0.1, 1.9)
    first_shift = normal_values(arg_keys[2], (C,), 0.3, 4.0, jnp.float32)
    query_weight = draw_query_weight(jax.random.fold_in(arg_keys[12], 71), 0)
    key_weight = draw_key_weight(jax.random.fold_in(arg_keys[12], 71), 0)
    value_weight = normal_values(arg_keys[5], (C, C), C ** -0.5, 0.3125)
    out_weight = normal_values(arg_keys[6], (C, C), C ** -0.5, 0.3125)
    out_bias = normal_values(arg_keys[7], (C,), 0.5, 6.0, jnp.float32)
    second_gain = jnp.clip(1.0 + 0.18 * jax.random.normal(arg_keys[8], (C,), jnp.float32), 0.1, 1.9)
    second_shift = normal_values(arg_keys[9], (C,), 0.3, 4.0, jnp.float32)
    up_weight = normal_values(arg_keys[10], (3, 3, 3, C, C), (27 * C // 8) ** -0.5, 0.15625)
    up_bias = normal_values(arg_keys[11], (C,), 0.5, 6.0, jnp.float32)
    return dict(latent=latent, first_gain=first_gain, first_shift=first_shift, query_weight=query_weight, key_weight=key_weight, value_weight=value_weight, out_weight=out_weight, out_bias=out_bias, second_gain=second_gain, second_shift=second_shift, up_weight=up_weight, up_bias=up_bias)


EPS = 1e-05

def group_norm(value, gain, shift):
    floats = value.astype(jnp.float32)
    shape = floats.shape
    grouped = floats.reshape(shape[:-1] + (GROUPS, shape[-1] // GROUPS))
    mean = lax.optimization_barrier(jnp.mean(grouped, axis=(0, 1, 2, 4), keepdims=True))
    spread = lax.optimization_barrier(jnp.mean(jnp.square(grouped - mean), axis=(0, 1, 2, 4), keepdims=True))
    normal_part = ((grouped - mean) * lax.rsqrt(spread + EPS)).reshape(shape)
    return normal_part * gain + shift

def upsample_taps(current, earlier, weight, bias):
    rows = current.shape[0] - 1
    cols = current.shape[1] - 1
    width = current.shape[2]
    time_taps = (((0, current), (2, earlier)), ((1, current),))
    space_taps = (((1, 0),), ((2, 0), (0, 1)))
    frame_list = []
    for odd_time in range(2):
        row_list = []
        for odd_row in range(2):
            col_list = []
            for odd_col in range(2):
                summed = jnp.zeros((rows * cols, width), jnp.float32)
                for time_tap, source in time_taps[odd_time]:
                    for row_tap, row_step in space_taps[odd_row]:
                        for col_tap, col_step in space_taps[odd_col]:
                            window = source[row_step:row_step + rows, col_step:col_step + cols].reshape(-1, width)
                            summed = summed + jnp.dot(window, weight[time_tap, row_tap, col_tap], preferred_element_type=jnp.float32)
                col_list.append((summed + bias).reshape(rows, cols, width))
            row_list.append(jnp.stack(col_list, axis=2).reshape(rows, 2 * cols, width))
        frame_list.append(jnp.stack(row_list, axis=1).reshape(2 * rows, 2 * cols, width))
    return jnp.stack(frame_list, axis=0)

def reference(latent, first_gain, first_shift, query_weight, key_weight, value_weight, out_weight, out_bias, second_gain, second_shift, up_weight, up_bias):
    frames, rows, cols, width = latent.shape
    normed = group_norm(latent, first_gain, first_shift).astype(jnp.bfloat16)
    flat = normed.reshape(-1, width)
    queries = jnp.dot(flat, query_weight, preferred_element_type=jnp.float32).astype(jnp.bfloat16).reshape(frames, rows, cols, width)
    keys = jnp.dot(flat, key_weight, preferred_element_type=jnp.float32).astype(jnp.bfloat16).reshape(frames, rows * cols, width)
    values = jnp.dot(flat, value_weight, preferred_element_type=jnp.float32).astype(jnp.bfloat16).reshape(frames, rows * cols, width)
    factor = width ** (-0.5)

    def one_frame(inputs):
        frame_queries, frame_keys, frame_values = inputs

        def one_row(row_queries):
            scores = jnp.dot(row_queries, frame_keys.T, preferred_element_type=jnp.float32) * factor
            highest = lax.optimization_barrier(jnp.max(scores, axis=-1, keepdims=True))
            weights = jnp.exp(scores - highest)
            totals = lax.optimization_barrier(jnp.sum(weights, axis=-1, keepdims=True))
            summed = jnp.dot(weights.astype(jnp.bfloat16), frame_values, preferred_element_type=jnp.float32)
            return (summed / totals).astype(jnp.bfloat16)
        return lax.map(one_row, frame_queries)
    attended = lax.map(one_frame, (queries, keys, values))
    branch = jnp.dot(attended.reshape(-1, width), out_weight, preferred_element_type=jnp.float32).reshape(latent.shape) + out_bias
    mixed = (latent.astype(jnp.float32) + branch).astype(jnp.bfloat16)
    activated = jax.nn.silu(group_norm(mixed, second_gain, second_shift)).astype(jnp.bfloat16)
    padded = jnp.pad(activated, ((1, 0), (0, 1), (0, 1), (0, 0)))

    def one_output(index):
        current = lax.dynamic_index_in_dim(padded, index + 1, 0, keepdims=False)
        earlier = lax.dynamic_index_in_dim(padded, index, 0, keepdims=False)
        return upsample_taps(current, earlier, up_weight, up_bias).astype(jnp.bfloat16)
    result = lax.map(one_output, jnp.arange(frames, dtype=jnp.int32))
    return result.reshape(2 * frames, 2 * rows, 2 * cols, width)
```

```python
import jax
import jax.numpy as jnp
from jax import lax
from jax.experimental import pallas as pl
from jax.experimental.pallas import tpu as pltpu
from jax.sharding import PartitionSpec as P

GROUPS = 32
EPS = 1e-05
LOG2E = 1.4426950408889634
MESH = pl.DeviceIdType.MESH
BF16 = jnp.bfloat16
F32 = jnp.float32

NSLOT = 8


def make_kernel(nf, nh, rows, cols, width):
    slab = rows * cols
    half = slab // 2
    group = 16
    nx = nh // group
    total = float(nf * nh * slab)
    per_group = width // GROUPS
    lanes = width // 128

    def kernel(
        lat, g1, s1, wq, wk, wv, wo, ob, g2, s2, wup, ub, out,
        kv, xq, q2, acc, part, partin, lse, lsein, w4, wupv, vec,
        st, curm, earm, act, stage, outv,
        ssem, rsem, rs_s, rs_r, ls_s, ls_r, sib_s, sib_r, misc_s, misc_r, loc, locw, outs,
    ):
        f = lax.axis_index("frames")
        h = lax.axis_index("height")
        xh = h // group
        k = h % group
        e = f * nx + xh

        def near(j):
            return (f, xh * group + (k + j) % group)

        def far(j):
            other = (e + j) % group
            return (other // nx, (other % nx) * group + k)

        right = near(2)
        left = near(group - 2)
        sibling = (f, xh * group + k + 1 - 2 * (k % 2))
        partner = (f, (h + group) % nh)
        above = (h + nh - 1) % nh
        below = (h + 1) % nh
        later = (f + 1) % nf
        sooner = (f + nf - 1) % nf

        barrier = pltpu.get_barrier_semaphore()

        def greet(dev):
            pl.semaphore_signal(barrier, inc=1, device_id=dev, device_id_type=MESH)

        own_copy = pltpu.make_async_copy(lat, kv.at[0, pl.ds(0, slab)], loc.at[0])
        own_copy.start()

        def greet_both(j, carry):
            greet(near(j))
            greet(far(j))
            return carry

        lax.fori_loop(1, group, greet_both, 0)
        for dev in ((f, above), (f, below), (later, above), (sooner, below)):
            greet(dev)

        small = [
            pltpu.make_async_copy(src, w4.at[i], loc.at[1 + i])
            for i, src in enumerate((wq, wk, wv, wo))
        ]
        small += [
            pltpu.make_async_copy(src, vec.at[i], loc.at[5 + i])
            for i, src in enumerate((g1, s1, ob, g2, s2, ub))
        ]
        for copy in small:
            copy.start()
        up_copy = pltpu.make_async_copy(wup, wupv, locw)

        def send(src, dst, ss, rs, dev):
            return pltpu.make_async_remote_copy(
                src_ref=src, dst_ref=dst, send_sem=ss, recv_sem=rs, device_id=dev, device_id_type=MESH
            )

        def ring(step, to_right):
            hop = step // 2
            source = 0 if hop == 0 else (2 * hop - 1 if to_right else 2 * hop)
            target = 7 if hop == 3 else (2 * hop + 1 if to_right else 2 * hop + 2)
            piece = step % 2 if hop < 3 else (0 if to_right else 1)
            at = pl.ds(piece * half, half)
            ss, rs = (rs_s, rs_r) if to_right else (ls_s, ls_r)
            return send(
                kv.at[source, at], kv.at[target, at], ss.at[step], rs.at[step], right if to_right else left
            )

        rings = {(s, d): ring(s, d) for s in range(7) for d in (True, False)}
        sibs = [
            send(kv.at[s, pl.ds(0, slab)], kv.at[s, pl.ds(slab, slab)], sib_s.at[s], sib_r.at[s], sibling)
            for s in range(NSLOT)
        ]
        to_partner = send(kv.at[0, pl.ds(0, slab)], xq, misc_s.at[0], misc_r.at[0], partner)

        own_copy.wait()
        pl.semaphore_wait(barrier, 2 * (group - 1) + 4)
        for s in (0, 1):
            rings[s, True].start()
            rings[s, False].start()
        to_partner.start()
        sibs[0].start()
        up_copy.start()

        def local_stats(x, slot):
            mean = jnp.sum(x, axis=0, keepdims=True) * (1.0 / slab)
            d = x - mean
            st[slot, 0] = jnp.concatenate([mean, jnp.sum(d * d, axis=0, keepdims=True)], axis=1)

        def exchange(slot, peer, count):
            def copy(j):
                return send(
                    st.at[slot, 0], st.at[slot, j], ssem.at[slot, j], rsem.at[slot, j], peer(j)
                )

            def begin(j, carry):
                copy(j).start()
                return carry

            def finish(j, carry):
                copy(j).wait()
                return carry

            lax.fori_loop(1, group, begin, 0)
            lax.fori_loop(1, group, finish, 0)
            means = [st[slot, j, :, 0:width] for j in range(group)]
            mean = sum(means) * (1.0 / group)
            m2 = sum(st[slot, j, :, width : 2 * width] for j in range(group))
            dev = sum((one - mean) * (one - mean) for one in means)
            return mean, m2 + count * dev

        grp_row = (lax.broadcasted_iota(jnp.int32, (width, width), 0) * 5462) >> 16
        grp_col = (lax.broadcasted_iota(jnp.int32, (width, width), 1) * 5462) >> 16
        same = jnp.where(grp_row == grp_col, 1.0, 0.0).astype(F32)

        def over_group(row):
            wide = jnp.broadcast_to(row, (8, width))
            return jnp.dot(
                wide, same, precision=lax.Precision.HIGHEST, preferred_element_type=F32
            )[0:1]

        def all_stats(slot):
            mean, m2 = exchange(slot, near, float(slab))
            st[slot + 1, 0] = jnp.concatenate([mean, m2], axis=1)
            mean, m2 = exchange(slot + 1, far, float(group * slab))
            gmean = over_group(mean) * (1.0 / per_group)
            d = mean - gmean
            gvar = over_group(m2 + total * d * d) * (1.0 / (per_group * total))
            return gmean, lax.rsqrt(gvar + EPS)

        own = kv[0, 0:slab].astype(F32)
        local_stats(own, 0)
        mean1, rstd1 = all_stats(0)

        for copy in small:
            copy.wait()

        scale1 = vec[0] * rstd1
        shift1 = vec[1]
        base1 = shift1 - mean1 * scale1
        key_scale = scale1 * (width**-0.5 * LOG2E)

        def make_queries(x, base):
            normed = ((x - mean1) * scale1 + shift1).astype(BF16)
            q = jnp.dot(normed, w4[0], preferred_element_type=F32).astype(BF16)
            t = lax.dot_general(q, w4[1], (((1,), (1,)), ((), ())), preferred_element_type=F32)
            q2[base : base + slab, :] = (t * key_scale).astype(BF16)

        state = {}

        def attend(who, first, count):
            base = who * slab
            keys = kv[first] if count == 1 else kv[first : first + count].reshape(count * 2 * slab, width)
            s = lax.dot_general(
                q2[base : base + slab, :], keys, (((1,), (1,)), ((), ())), preferred_element_type=F32
            )
            top = jnp.max(s, axis=-1, keepdims=True)
            if who in state:
                m, l = state[who]
                top = jnp.maximum(m, top)
                alpha = jnp.exp2(m - top)
            p = jnp.exp2(s - top).astype(BF16)
            psum = jnp.sum(p.astype(F32), axis=-1, keepdims=True)
            o = jnp.dot(p, keys, preferred_element_type=F32)
            if who in state:
                psum = l * alpha + psum
                o = acc[base : base + slab, :] * alpha + o
            acc[base : base + slab, :] = o
            state[who] = (top, psum)

        def finished(who):
            m, l = state[who]
            base = who * slab
            mean_key = acc[base : base + slab, :] / l
            return mean_key * scale1 + base1, m + jnp.log(l) * LOG2E

        diag = lax.broadcasted_iota(jnp.int32, (slab, width), 0) == lax.broadcasted_iota(
            jnp.int32, (slab, width), 1
        )

        OWN, OTHER = 0, 1
        forward_pair(rings, 0)
        make_queries(own, 0)
        to_partner.wait_recv()
        make_queries(xq[...].astype(F32), slab)
        forward_pair(rings, 1)
        sibs[1].start()
        sibs[2].start()
        sibs[0].wait_recv()
        attend(OTHER, 0, 1)
        attend(OWN, 0, 1)
        forward_pair(rings, 2)
        sibs[1].wait_recv()
        sibs[2].wait_recv()
        attend(OTHER, 1, 2)
        forward_pair(rings, 3)
        sibs[3].start()
        sibs[4].start()
        attend(OWN, 1, 2)
        sibs[3].wait_recv()
        sibs[4].wait_recv()
        forward_pair(rings, 4)
        attend(OTHER, 3, 2)
        attend(OWN, 3, 2)
        forward_pair(rings, 5)
        sibs[5].start()
        sibs[6].start()
        sibs[5].wait_recv()
        sibs[6].wait_recv()
        attend(OTHER, 5, 2)
        forward_pair(rings, 6)
        sibs[7].start()
        sibs[7].wait_recv()
        attend(OTHER, 7, 1)

        o, w = finished(OTHER)
        part[...] = o.astype(BF16)
        lse[...] = jnp.sum(jnp.where(diag, w, 0.0), axis=0, keepdims=True)
        part_copy = send(part, partin, misc_s.at[1], misc_r.at[1], partner)
        lse_copy = send(lse, lsein, misc_s.at[2], misc_r.at[2], partner)
        part_copy.start()
        lse_copy.start()
        attend(OWN, 5, 2)
        attend(OWN, 7, 1)
        o1, w1 = finished(OWN)
        lse_copy.wait_recv()
        w2 = jnp.sum(jnp.where(diag, lsein[...], 0.0), axis=1, keepdims=True)
        top = jnp.maximum(w1, w2)
        e1 = jnp.exp2(w1 - top)
        e2 = jnp.exp2(w2 - top)
        inv = 1.0 / (e1 + e2)
        o1 = o1 * (e1 * inv)
        part_copy.wait_recv()
        o = (o1 + partin[...].astype(F32) * (e2 * inv)).astype(BF16)
        attended = jnp.dot(o, w4[2], preferred_element_type=F32).astype(BF16)
        mixed = jnp.dot(attended, w4[3], preferred_element_type=F32) + vec[2] + kv[0, 0:slab].astype(F32)
        mixed = mixed.astype(BF16)
        curm[0:slab, :] = mixed
        top_row = pl.ds(0, cols)
        low_row = pl.ds(slab, cols)
        halos = [
            send(curm.at[pl.ds(0, slab)], earm.at[pl.ds(0, slab)], misc_s.at[3], misc_r.at[3], (later, h)),
            send(curm.at[top_row], curm.at[low_row], misc_s.at[4], misc_r.at[4], (f, above)),
            send(curm.at[top_row], earm.at[low_row], misc_s.at[5], misc_r.at[5], (later, above)),
        ]
        for copy in halos:
            copy.start()
        local_stats(mixed.astype(F32), 2)
        mean2, rstd2 = all_stats(2)
        scale2 = vec[3] * rstd2
        shift2 = vec[4]

        last_col = lax.broadcasted_iota(jnp.int32, (cols, width), 0) == cols - 1

        def activate(src, which, r, keep):
            x = src[r * cols : (r + 1) * cols, :].astype(F32)
            v = (x - mean2) * scale2 + shift2
            y = v / (1.0 + jnp.exp(-v))
            if keep is not None:
                y = jnp.where(keep, y, 0.0)
            act[which, 0, r * cols : (r + 1) * cols, :] = y.astype(BF16)
            y = jnp.where(last_col, 0.0, pltpu.roll(y, cols - 1, 0))
            act[which, 1, r * cols : (r + 1) * cols, :] = y.astype(BF16)

        has_below = h < nh - 1
        has_sooner = f > 0
        for r in range(rows):
            activate(curm, 0, r, None)
        for copy in halos:
            copy.wait_recv()
        activate(curm, 0, rows, has_below)
        for r in range(rows):
            activate(earm, 1, r, has_sooner)
        activate(earm, 1, rows, jnp.logical_and(has_below, has_sooner))
        up_copy.wait()

        taps = (((0, 1),), ((0, 2), (1, 0)))
        out_copies = []
        for b in range(2):
            for c in range(2):
                wins = [(rs, cs, q, r) for rs, q in taps[b] for cs, r in taps[c]]

                def windows(which):
                    parts = [act[which, cs, rs * cols : rs * cols + slab, :] for rs, cs, _, _ in wins]
                    return parts[0] if len(parts) == 1 else jnp.concatenate(parts, axis=1)

                def weights(p):
                    parts = [wupv[p, q, r] for _, _, q, r in wins]
                    return parts[0] if len(parts) == 1 else jnp.concatenate(parts, axis=0)

                current = windows(0)
                both = jnp.dot(
                    current,
                    jnp.concatenate([weights(0), weights(1)], axis=1),
                    preferred_element_type=F32,
                )
                y0 = both[:, 0:width] + jnp.dot(windows(1), weights(2), preferred_element_type=F32)
                for a, y in ((0, y0), (1, both[:, width:])):
                    y = y + vec[5]
                    for i in range(rows):
                        for n in range(lanes):
                            stage[a, i, n, pl.ds(c, cols, stride=2), :] = y[
                                i * cols : (i + 1) * cols, n * 128 : (n + 1) * 128
                            ]
            for a in range(2):
                for i in range(rows):
                    line = 2 * i + b
                    for n in range(lanes):
                        outv[a, line, :, n * 128 : (n + 1) * 128] = stage[a, i, n].astype(BF16)
                    copy = pltpu.make_async_copy(outv.at[a, line], out.at[a, line], outs.at[a, line])
                    copy.start()
                    out_copies.append(copy)

        for copy in out_copies:
            copy.wait()
        for copy in rings.values():
            copy.wait_send()
        for copy in sibs:
            copy.wait_send()
        to_partner.wait_send()
        part_copy.wait_send()
        lse_copy.wait_send()
        for copy in halos:
            copy.wait_send()

    def forward_pair(rings, step):
        for d in (True, False):
            rings[step, d].wait_recv()
            follow = step + 2
            if follow < 6:
                rings[follow, d].start()
            elif follow == 6 and d:
                rings[follow, d].start()
            elif follow == 7 and not d:
                rings[6, d].start()

    slab2 = 2 * slab
    dma = pltpu.SemaphoreType.DMA
    scratch = [
        pltpu.VMEM((NSLOT, slab2, width), BF16),
        pltpu.VMEM((slab, width), BF16),
        pltpu.VMEM((slab2, width), BF16),
        pltpu.VMEM((slab2, width), F32),
        pltpu.VMEM((slab, width), BF16),
        pltpu.VMEM((slab, width), BF16),
        pltpu.VMEM((1, width), F32),
        pltpu.VMEM((1, width), F32),
        pltpu.VMEM((4, width, width), BF16),
        pltpu.VMEM((3, 3, 3, width, width), BF16),
        pltpu.VMEM((6, 1, width), F32),
        pltpu.VMEM((4, group, 1, 2 * width), F32),
        pltpu.VMEM((slab + cols, width), BF16),
        pltpu.VMEM((slab + cols, width), BF16),
        pltpu.VMEM((2, 2, slab + cols, width), BF16),
        pltpu.VMEM((2, rows, lanes, 2 * cols, 128), F32),
        pltpu.VMEM((2, 2 * rows, 2 * cols, width), BF16),
        dma((4, group)),
        dma((4, group)),
        dma((7,)),
        dma((7,)),
        dma((7,)),
        dma((7,)),
        dma((NSLOT,)),
        dma((NSLOT,)),
        dma((6,)),
        dma((6,)),
        dma((11,)),
        dma,
        dma((2, 2 * rows)),
    ]
    return kernel, scratch


def solution(mesh):
    nf, nh = mesh.shape["frames"], mesh.shape["height"]

    def local(
        latent, first_gain, first_shift, query_weight, key_weight, value_weight, out_weight, out_bias,
        second_gain, second_shift, up_weight, up_bias,
    ):
        _, rows, cols, width = latent.shape
        kernel, scratch = make_kernel(nf, nh, rows, cols, width)

        def row(v):
            return v.reshape(1, width)

        out = pl.pallas_call(
            kernel,
            out_shape=jax.ShapeDtypeStruct((2, 2 * rows, 2 * cols, width), BF16),
            in_specs=[pl.BlockSpec(memory_space=pl.ANY)] * 12,
            out_specs=pl.BlockSpec(memory_space=pl.ANY),
            scratch_shapes=scratch,
            compiler_params=pltpu.CompilerParams(
                collective_id=0, has_side_effects=True, vmem_limit_bytes=56 * 1024 * 1024
            ),
            name="decoder_window",
        )(
            latent.reshape(rows * cols, width),
            row(first_gain), row(first_shift),
            query_weight, key_weight, value_weight, out_weight,
            row(out_bias), row(second_gain), row(second_shift),
            up_weight, row(up_bias),
        )
        return out

    whole = P("frames", "height", None, None)
    return jax.shard_map(
        local, mesh=mesh, in_specs=(whole,) + (P(),) * 11, out_specs=whole, check_vma=False
    )
```

```python
import jax
import jax.numpy as jnp
from jax import lax
from jax.experimental import pallas as pl
from jax.experimental.pallas import tpu as pltpu
from jax.sharding import PartitionSpec as P

GROUPS = 32
EPS = 1e-05
LOG2E = 1.4426950408889634
MESH = pl.DeviceIdType.MESH
BF16 = jnp.bfloat16
F32 = jnp.float32

NSLOT = 8
PIECES = 4


def make_kernel(nf, nh, rows, cols, width):
    slab = rows * cols
    piece = slab // PIECES
    steps = 3 * PIECES + PIECES // 2
    group = 16
    nx = nh // group
    total = float(nf * nh * slab)
    per_group = width // GROUPS
    lanes = width // 128

    def kernel(
        lat, g1, s1, wq, wk, wv, wo, ob, g2, s2, wup, ub, out,
        kv, xq, q2, acc, part, partin, lse, lsein, w4, wupv,
        g1v, s1v, obv, g2v, s2v, ubv, same,
        st, curm, earm, act, stage,
        st_s, st_r, kv_s, ring_r, sib_r, tail_s, misc_r, lse_s, loc, locv,
    ):
        vec = (g1v, s1v, obv, g2v, s2v, ubv)
        f = lax.axis_index("frames")
        h = lax.axis_index("height")
        xh = h // group
        k = h % group
        e = f * nx + xh

        def near(j):
            return (f, xh * group + (k + j) % group)

        def far(j):
            other = (e + j) % group
            return (other // nx, (other % nx) * group + k)

        right = near(2)
        left = near(group - 2)
        sibling = (f, xh * group + k + 1 - 2 * (k % 2))
        partner = (f, (h + group) % nh)
        above = (h + nh - 1) % nh
        below = (h + 1) % nh
        later = (f + 1) % nf
        sooner = (f + nf - 1) % nf

        def vrow(i):
            return vec[i][...].reshape(1, width)

        barrier = pltpu.get_barrier_semaphore()

        def greet(dev):
            pl.semaphore_signal(barrier, inc=1, device_id=dev, device_id_type=MESH)

        own_copy = pltpu.make_async_copy(lat, kv.at[0, pl.ds(0, slab)], loc.at[0])
        own_copy.start()

        def greet_both(j, carry):
            greet(near(j))
            greet(far(j))
            return carry

        lax.fori_loop(1, group, greet_both, 0)
        for dev in ((f, above), (f, below), (later, above), (sooner, below)):
            greet(dev)

        small = [
            pltpu.make_async_copy(src, w4.at[i], loc.at[1]) for i, src in enumerate((wq, wk, wv, wo))
        ]
        rows_in = [
            pltpu.make_async_copy(src, dst, locv.at[i])
            for i, (src, dst) in enumerate(zip((g1, s1, ob, g2, s2, ub), vec))
        ]
        for copy in small + rows_in:
            copy.start()
        up_copy = pltpu.make_async_copy(wup, wupv, loc.at[2])

        def send(src, dst, ss, rs, dev):
            return pltpu.make_async_remote_copy(
                src_ref=src, dst_ref=dst, send_sem=ss, recv_sem=rs, device_id=dev, device_id_type=MESH
            )

        def took(sem, size):
            pltpu.make_async_copy(size, size, sem).wait()

        def ring(step, to_right):
            hop = step // PIECES
            source = 0 if hop == 0 else (2 * hop - 1 if to_right else 2 * hop)
            target = 7 if hop == 3 else (2 * hop + 1 if to_right else 2 * hop + 2)
            at = pl.ds(((step % PIECES) + (0 if hop < 3 or to_right else PIECES // 2)) * piece, piece)
            return send(
                kv.at[source, at], kv.at[target, at], kv_s, ring_r.at[step], right if to_right else left
            )

        rings = {(s, d): ring(s, d) for s in range(steps) for d in (True, False)}

        def pass_on(first, last):
            for s in range(first, last):
                took(ring_r.at[s], kv.at[0, pl.ds(0, 2 * piece)])
                for d in (True, False):
                    onward = s + PIECES
                    if onward >= 3 * PIECES and not d:
                        onward -= PIECES // 2
                        if onward < 3 * PIECES:
                            continue
                    if onward < steps:
                        rings[onward, d].start()

        sibs = [
            send(kv.at[s, pl.ds(0, slab)], kv.at[s, pl.ds(slab, slab)], kv_s, sib_r.at[(s + 1) // 2], sibling)
            for s in range(NSLOT)
        ]
        to_partner = send(kv.at[0, pl.ds(0, slab)], xq, kv_s, misc_r.at[0], partner)

        def local_stats(x, slot):
            mean = jnp.sum(x, axis=0, keepdims=True) * (1.0 / slab)
            d = x - mean
            st[slot, 0] = jnp.concatenate([mean, jnp.sum(d * d, axis=0, keepdims=True)], axis=1)

        def messages(slot, peer):
            return [
                send(st.at[slot, 0], st.at[slot, j], st_s.at[slot], st_r.at[slot], peer(j))
                for j in range(1, group)
            ]

        def start(copies):
            for copy in copies:
                copy.start()

        def told(slot):
            took(st_r.at[slot], st.at[slot, pl.ds(1, group - 1)])

        def mates(i):
            took(sib_r.at[i], kv.at[0] if 0 < i < 4 else kv.at[0, pl.ds(0, slab)])

        def merged(slot, count):
            means = [st[slot, j, :, 0:width] for j in range(group)]
            mean = sum(means) * (1.0 / group)
            m2 = sum(st[slot, j, :, width : 2 * width] for j in range(group))
            return mean, m2 + count * sum((one - mean) * (one - mean) for one in means)

        def merge_to(slot, target, count):
            mean, m2 = merged(slot, count)
            st[target, 0] = jnp.concatenate([mean, m2], axis=1)

        line = lax.broadcasted_iota(jnp.int32, (16, width), 0)

        def over_group(row):
            high = row.astype(BF16).astype(F32)
            rest = row - high
            middle = rest.astype(BF16).astype(F32)
            pieces = jnp.where(line == 0, high, jnp.where(line == 1, middle, rest - middle))
            pieces = jnp.where(line < 3, pieces, 0.0).astype(BF16)
            sums = jnp.dot(pieces, same[...], preferred_element_type=F32)
            return jnp.sum(sums, axis=0, keepdims=True)

        def group_stats(slot):
            mean, m2 = merged(slot, float(group * slab))
            gmean = over_group(mean) * (1.0 / per_group)
            d = mean - gmean
            gvar = over_group(m2 + total * d * d) * (1.0 / (per_group * total))
            return gmean, lax.rsqrt(gvar + EPS)

        near1, far1 = messages(0, near), messages(1, far)
        far2, near2 = messages(2, far), messages(3, near)

        own_copy.wait()
        own = kv[0, 0:slab].astype(F32)
        local_stats(own, 0)
        grp_row = (lax.broadcasted_iota(jnp.int32, (width, width), 0) * 5462) >> 16
        grp_col = (lax.broadcasted_iota(jnp.int32, (width, width), 1) * 5462) >> 16
        same[...] = jnp.where(grp_row == grp_col, 1.0, 0.0).astype(BF16)
        pl.semaphore_wait(barrier, 2 * (group - 1) + 4)
        start(near1)
        for s in range(PIECES):
            rings[s, True].start()
            rings[s, False].start()
        to_partner.start()
        sibs[0].start()
        up_copy.start()
        took(loc.at[1], w4)
        for copy in rows_in:
            copy.wait()
        value_out = jnp.dot(w4[2], w4[3], preferred_element_type=F32).astype(BF16)
        w4[2] = value_out
        told(0)
        merge_to(0, 1, float(slab))
        start(far1)
        pass_on(0, 4)
        start(sibs[1:3])
        pass_on(4, 5)
        told(1)
        mean1, rstd1 = group_stats(1)
        pass_on(5, 6)
        scale1 = vrow(0) * rstd1
        shift1 = vrow(1)
        base1 = shift1 - mean1 * scale1
        key_scale = scale1 * (width**-0.5 * LOG2E)

        def make_queries(x, base):
            normed = ((x - mean1) * scale1 + shift1).astype(BF16)
            q = jnp.dot(normed, w4[0], preferred_element_type=F32).astype(BF16)
            t = lax.dot_general(q, w4[1], (((1,), (1,)), ((), ())), preferred_element_type=F32)
            q2[base : base + slab, :] = (t * key_scale).astype(BF16)

        state = {}

        def attend_rows(base, n, m, l, first, count):
            at = slice(base, base + n)
            keys = kv[first : first + count].reshape(count * 2 * slab, width)
            s = lax.dot_general(
                q2[at, :], keys, (((1,), (1,)), ((), ())), preferred_element_type=F32
            )
            top = jnp.max(s, axis=-1, keepdims=True)
            if m is not None:
                top = jnp.maximum(m, top)
                alpha = jnp.exp2(m - top)
            p = jnp.exp2(s - top).astype(BF16)
            psum = jnp.sum(p.astype(F32), axis=-1, keepdims=True)
            o = jnp.dot(p, keys, preferred_element_type=F32)
            if m is not None:
                psum = l * alpha + psum
                o = acc[at, :] * alpha + o
            acc[at, :] = o
            return top, psum

        def attend(who, first, count):
            m, l = state.get(who, (None, None))
            state[who] = attend_rows(who * slab, slab, m, l, first, count)

        def finished(base, n, m, l):
            mean_key = acc[base : base + n, :] / l
            return (mean_key * scale1 + base1).astype(BF16), m + jnp.log(l) * LOG2E

        diag = lax.broadcasted_iota(jnp.int32, (slab, width), 0) == lax.broadcasted_iota(
            jnp.int32, (slab, width), 1
        )

        OWN, OTHER = 0, 1
        make_queries(own, 0)
        pass_on(6, 7)
        to_partner.wait_recv()
        make_queries(xq[...].astype(F32), slab)
        pass_on(7, 8)
        start(sibs[3:5])
        mates(0)
        attend(OTHER, 0, 1)
        mates(1)
        attend(OTHER, 1, 2)
        pass_on(8, 9)
        mates(2)
        attend(OTHER, 3, 2)
        pass_on(9, 10)
        attend(OWN, 0, 1)
        pass_on(10, 11)
        attend(OWN, 1, 2)
        pass_on(11, 12)
        start(sibs[5:7])
        attend(OWN, 3, 2)
        pass_on(12, 13)
        mates(3)
        attend(OTHER, 5, 2)
        pass_on(13, 14)
        sibs[7].start()
        mates(4)
        halfway = slab // 2
        halves = [slice(0, halfway), slice(halfway, slab)]
        part_copies = [
            send(part.at[pl.ds(i * halfway, halfway)], partin.at[pl.ds(i * halfway, halfway)], tail_s, misc_r.at[1 + i], partner)
            for i in range(2)
        ]
        lse_copy = send(lse, lsein, lse_s, misc_r.at[3], partner)
        m, l = state[OTHER]
        weights = []
        for i, at in enumerate(halves):
            top, total_l = attend_rows(slab + i * halfway, halfway, m[at], l[at], 7, 1)
            part[at, :], w = finished(slab + i * halfway, halfway, top, total_l)
            weights.append(w)
            if i == 1:
                w = jnp.concatenate(weights, axis=0)
                lse[...] = jnp.sum(jnp.where(diag, w, 0.0), axis=0, keepdims=True)
                lse_copy.start()
            part_copies[i].start()
        attend(OWN, 5, 2)
        attend(OWN, 7, 1)
        o1, w1 = finished(0, slab, *state[OWN])
        y1 = jnp.dot(o1, w4[2], preferred_element_type=F32)
        base = kv[0, 0:slab].astype(F32) + vrow(2)
        lse_copy.wait_recv()
        w2 = jnp.sum(jnp.where(diag, lsein[...], 0.0), axis=1, keepdims=True)
        top = jnp.maximum(w1, w2)
        e1 = jnp.exp2(w1 - top)
        e2 = jnp.exp2(w2 - top)
        inv = 1.0 / (e1 + e2)
        base = base + y1 * (e1 * inv)
        e2 = e2 * inv
        mixed = []
        for i, at in enumerate(halves):
            part_copies[i].wait_recv()
            y2 = jnp.dot(partin[at, :], w4[2], preferred_element_type=F32)
            mixed.append((base[at] + y2 * e2[at]).astype(BF16))
        mixed = jnp.concatenate(mixed, axis=0)
        curm[0:slab, :] = mixed
        top_row = pl.ds(0, cols)
        low_row = pl.ds(slab, cols)
        halos = [
            send(curm.at[pl.ds(0, slab)], earm.at[pl.ds(0, slab)], tail_s, misc_r.at[4], (later, h)),
            send(curm.at[top_row], curm.at[low_row], tail_s, misc_r.at[4], (f, above)),
            send(curm.at[top_row], earm.at[low_row], tail_s, misc_r.at[4], (later, above)),
        ]
        local_stats(mixed.astype(F32), 2)
        start(far2)
        start(halos)
        told(2)
        merge_to(2, 3, float(slab))
        start(near2)
        told(3)
        mean2, rstd2 = group_stats(3)
        scale2 = vrow(3) * rstd2
        shift2 = vrow(4)

        last_col = lax.broadcasted_iota(jnp.int32, (cols, width), 0) == cols - 1

        def activate(src, which, r, keep):
            x = src[r * cols : (r + 1) * cols, :].astype(F32)
            v = (x - mean2) * scale2 + shift2
            y = v / (1.0 + jnp.exp(-v))
            if keep is not None:
                y = jnp.where(keep, y, 0.0)
            act[which, 0, r * cols : (r + 1) * cols, :] = y.astype(BF16)
            y = jnp.where(last_col, 0.0, pltpu.roll(y, cols - 1, 0))
            act[which, 1, r * cols : (r + 1) * cols, :] = y.astype(BF16)

        has_below = h < nh - 1
        has_sooner = f > 0
        for r in range(rows):
            activate(curm, 0, r, None)
        took(misc_r.at[4], kv.at[0])
        activate(curm, 0, rows, has_below)
        for r in range(rows):
            activate(earm, 1, r, has_sooner)
        activate(earm, 1, rows, jnp.logical_and(has_below, has_sooner))
        up_copy.wait()

        taps = (((0, 1),), ((0, 2), (1, 0)))
        for b in range(2):
            for c in range(2):
                wins = [(rs, cs, q, r) for rs, q in taps[b] for cs, r in taps[c]]

                def windows(which):
                    parts = [act[which, cs, rs * cols : rs * cols + slab, :] for rs, cs, _, _ in wins]
                    return parts[0] if len(parts) == 1 else jnp.concatenate(parts, axis=1)

                def weights(p):
                    parts = [wupv[p, q, r] for _, _, q, r in wins]
                    return parts[0] if len(parts) == 1 else jnp.concatenate(parts, axis=0)

                current = windows(0)
                both = jnp.dot(
                    current,
                    jnp.concatenate([weights(0), weights(1)], axis=1),
                    preferred_element_type=F32,
                )
                y0 = both[:, 0:width] + jnp.dot(windows(1), weights(2), preferred_element_type=F32)
                for a, y in ((0, y0), (1, both[:, width:])):
                    y = y + vrow(5)
                    for i in range(rows):
                        for n in range(lanes):
                            stage[a, i, n, pl.ds(c, cols, stride=2), :] = y[
                                i * cols : (i + 1) * cols, n * 128 : (n + 1) * 128
                            ]
            for a in range(2):
                for i in range(rows):
                    for n in range(lanes):
                        out[a, 2 * i + b, :, n * 128 : (n + 1) * 128] = stage[a, i, n].astype(BF16)

        took(kv_s, kv)
        took(tail_s, act.at[0])
        lse_copy.wait_send()
        for slot in range(4):
            took(st_s.at[slot], st.at[slot, pl.ds(1, group - 1)])

    slab2 = 2 * slab
    dma = pltpu.SemaphoreType.DMA
    scratch = [
        pltpu.VMEM((NSLOT, slab2, width), BF16),
        pltpu.VMEM((slab, width), BF16),
        pltpu.VMEM((slab2, width), BF16),
        pltpu.VMEM((slab2, width), F32),
        pltpu.VMEM((slab, width), BF16),
        pltpu.VMEM((slab, width), BF16),
        pltpu.VMEM((1, width), F32),
        pltpu.VMEM((1, width), F32),
        pltpu.VMEM((4, width, width), BF16),
        pltpu.VMEM((3, 3, 3, width, width), BF16),
        *[pltpu.VMEM((width,), F32)] * 6,
        pltpu.VMEM((width, width), BF16),
        pltpu.VMEM((4, group, 1, 2 * width), F32),
        pltpu.VMEM((slab + cols, width), BF16),
        pltpu.VMEM((slab + cols, width), BF16),
        pltpu.VMEM((2, 2, slab + cols, width), BF16),
        pltpu.VMEM((2, rows, lanes, 2 * cols, 128), F32),
        dma((4,)),
        dma((4,)),
        dma,
        dma((steps,)),
        dma((5,)),
        dma,
        dma((5,)),
        dma,
        dma((3,)),
        dma((6,)),
    ]
    return kernel, scratch


def solution(mesh):
    nf, nh = mesh.shape["frames"], mesh.shape["height"]

    def local(
        latent, first_gain, first_shift, query_weight, key_weight, value_weight, out_weight, out_bias,
        second_gain, second_shift, up_weight, up_bias,
    ):
        _, rows, cols, width = latent.shape
        kernel, scratch = make_kernel(nf, nh, rows, cols, width)

        out = pl.pallas_call(
            kernel,
            out_shape=pltpu.VMEM((2, 2 * rows, 2 * cols, width), BF16),
            in_specs=[pl.BlockSpec(memory_space=pl.ANY)] * 12,
            out_specs=pl.BlockSpec(memory_space=pltpu.VMEM),
            scratch_shapes=scratch,
            compiler_params=pltpu.CompilerParams(
                collective_id=0, has_side_effects=True, vmem_limit_bytes=56 * 1024 * 1024
            ),
            name="decoder_window",
        )(
            latent.reshape(rows * cols, width),
            first_gain, first_shift,
            query_weight, key_weight, value_weight, out_weight,
            out_bias, second_gain, second_shift,
            up_weight, up_bias,
        )
        return out

    whole = P("frames", "height", None, None)
    return jax.shard_map(
        local, mesh=mesh, in_specs=(whole,) + (P(),) * 11, out_specs=whole, check_vma=False
    )
```

```python
import jax
import jax.numpy as jnp
from jax import lax
from jax.experimental import pallas as pl
from jax.experimental.pallas import tpu as pltpu
from jax.sharding import PartitionSpec as P

GROUPS = 32
EPS = 1e-05
LOG2E = 1.4426950408889634
MESH = pl.DeviceIdType.MESH
BF16 = jnp.bfloat16
F32 = jnp.float32

NSLOT = 8
PIECES = 4


def make_kernel(nf, nh, rows, cols, width):
    slab = rows * cols
    piece = slab // PIECES
    steps = 3 * PIECES + PIECES // 2
    group = 16
    nx = nh // group
    total = float(nf * nh * slab)
    per_group = width // GROUPS
    lanes = width // 128

    def kernel(
        lat, g1, s1, wq, wk, wv, wo, ob, g2, s2, wup, ub, out,
        kv, xq, q2, acc, part, partin, lse, lsein, w4, wupv,
        g1v, s1v, obv, g2v, s2v, ubv, same,
        st, curm, earm, act, stage,
        st_s, st_r, kv_s, ring_r, sib_r, tail_s, misc_r, lse_s, loc, locv,
    ):
        vec = (g1v, s1v, obv, g2v, s2v, ubv)
        f = lax.axis_index("frames")
        h = lax.axis_index("height")
        xh = h // group
        k = h % group
        e = f * nx + xh

        def near(j):
            return (f, xh * group + (k + j) % group)

        def far(j):
            other = (e + j) % group
            return (other // nx, (other % nx) * group + k)

        right = near(2)
        left = near(group - 2)
        sibling = (f, xh * group + k + 1 - 2 * (k % 2))
        partner = (f, (h + group) % nh)
        above = (h + nh - 1) % nh
        below = (h + 1) % nh
        later = (f + 1) % nf

        def vrow(i):
            return vec[i][...].reshape(1, width)

        barrier = pltpu.get_barrier_semaphore()

        def greet(dev):
            pl.semaphore_signal(barrier, inc=1, device_id=dev, device_id_type=MESH)

        own_copy = pltpu.make_async_copy(lat, kv.at[0, pl.ds(0, slab)], loc.at[0])
        own_copy.start()

        def greet_both(j, carry):
            greet(near(j))
            greet(far(j))
            return carry

        lax.fori_loop(1, group, greet_both, 0)
        for dev in ((f, above), (f, below)):
            greet(dev)

        small = [
            pltpu.make_async_copy(src, w4.at[i], loc.at[1]) for i, src in enumerate((wq, wk, wv, wo))
        ]
        rows_in = [
            pltpu.make_async_copy(src, dst, locv.at[i])
            for i, (src, dst) in enumerate(zip((g1, s1, ob, g2, s2, ub), vec))
        ]
        for copy in small + rows_in:
            copy.start()
        up_copy = pltpu.make_async_copy(wup, wupv, loc.at[2])

        def send(src, dst, ss, rs, dev):
            return pltpu.make_async_remote_copy(
                src_ref=src, dst_ref=dst, send_sem=ss, recv_sem=rs, device_id=dev, device_id_type=MESH
            )

        def took(sem, size):
            pltpu.make_async_copy(size, size, sem).wait()

        def ring(step, to_right):
            hop = step // PIECES
            source = 0 if hop == 0 else (2 * hop - 1 if to_right else 2 * hop)
            target = 7 if hop == 3 else (2 * hop + 1 if to_right else 2 * hop + 2)
            at = pl.ds(((step % PIECES) + (0 if hop < 3 or to_right else PIECES // 2)) * piece, piece)
            return send(
                kv.at[source, at], kv.at[target, at], kv_s, ring_r.at[step], right if to_right else left
            )

        rings = {(s, d): ring(s, d) for s in range(steps) for d in (True, False)}

        def pass_on(first, last):
            for s in range(first * PIECES // 4, last * PIECES // 4):
                took(ring_r.at[s], kv.at[0, pl.ds(0, 2 * piece)])
                for d in (True, False):
                    onward = s + PIECES
                    if onward >= 3 * PIECES and not d:
                        onward -= PIECES // 2
                        if onward < 3 * PIECES:
                            continue
                    if onward < steps:
                        rings[onward, d].start()

        sibs = [
            send(kv.at[s, pl.ds(0, slab)], kv.at[s, pl.ds(slab, slab)], kv_s, sib_r.at[(s + 1) // 2], sibling)
            for s in range(NSLOT)
        ]
        to_partner = send(kv.at[0, pl.ds(0, slab)], xq, kv_s, misc_r.at[0], partner)

        def local_stats(x, slot):
            mean = jnp.sum(x, axis=0, keepdims=True) * (1.0 / slab)
            d = x - mean
            st[slot, 0] = jnp.concatenate([mean, jnp.sum(d * d, axis=0, keepdims=True)], axis=1)

        def messages(slot, peer):
            return [
                send(st.at[slot, 0], st.at[slot, j], st_s.at[slot], st_r.at[slot], peer(j))
                for j in sorted(range(1, group), key=lambda j: abs(j - group // 2))
            ]

        def start(copies):
            for copy in copies:
                copy.start()

        def told(slot):
            took(st_r.at[slot], st.at[slot, pl.ds(1, group - 1)])

        def mates(i):
            took(sib_r.at[i], kv.at[0] if 0 < i < 4 else kv.at[0, pl.ds(0, slab)])

        def merged(slot, count):
            means = [st[slot, j, :, 0:width] for j in range(group)]
            mean = sum(means) * (1.0 / group)
            m2 = sum(st[slot, j, :, width : 2 * width] for j in range(group))
            return mean, m2 + count * sum((one - mean) * (one - mean) for one in means)

        def merge_to(slot, target, count):
            mean, m2 = merged(slot, count)
            st[target, 0] = jnp.concatenate([mean, m2], axis=1)

        line = lax.broadcasted_iota(jnp.int32, (16, width), 0)

        def over_group(row):
            high = row.astype(BF16).astype(F32)
            rest = row - high
            middle = rest.astype(BF16).astype(F32)
            pieces = jnp.where(line == 0, high, jnp.where(line == 1, middle, rest - middle))
            pieces = jnp.where(line < 3, pieces, 0.0).astype(BF16)
            sums = jnp.dot(pieces, same[...], preferred_element_type=F32)
            return jnp.sum(sums, axis=0, keepdims=True)

        def group_stats(slot):
            mean, m2 = merged(slot, float(group * slab))
            gmean = over_group(mean) * (1.0 / per_group)
            d = mean - gmean
            gvar = over_group(m2 + total * d * d) * (1.0 / (per_group * total))
            return gmean, lax.rsqrt(gvar + EPS)

        near1, far1 = messages(0, near), messages(1, far)
        far2, near2 = messages(2, far), messages(3, near)

        own_copy.wait()
        own = kv[0, 0:slab].astype(F32)
        local_stats(own, 0)
        grp_row = (lax.broadcasted_iota(jnp.int32, (width, width), 0) * 5462) >> 16
        grp_col = (lax.broadcasted_iota(jnp.int32, (width, width), 1) * 5462) >> 16
        same[...] = jnp.where(grp_row == grp_col, 1.0, 0.0).astype(BF16)
        pl.semaphore_wait(barrier, 2 * (group - 1) + 2)
        start(near1)
        for s in range(PIECES):
            rings[s, True].start()
            rings[s, False].start()
        to_partner.start()
        sibs[0].start()
        up_copy.start()
        took(loc.at[1], w4)
        for copy in rows_in:
            copy.wait()
        value_out = jnp.dot(w4[2], w4[3], preferred_element_type=F32).astype(BF16)
        w4[2] = value_out
        told(0)
        merge_to(0, 1, float(slab))
        start(far1)
        pass_on(0, 4)
        start(sibs[1:3])
        pass_on(4, 5)
        told(1)
        mean1, rstd1 = group_stats(1)
        pass_on(5, 6)
        scale1 = vrow(0) * rstd1
        shift1 = vrow(1)
        base1 = shift1 - mean1 * scale1
        key_scale = scale1 * (width**-0.5 * LOG2E)

        def make_queries(x, base):
            normed = ((x - mean1) * scale1 + shift1).astype(BF16)
            q = jnp.dot(normed, w4[0], preferred_element_type=F32).astype(BF16)
            t = lax.dot_general(q, w4[1], (((1,), (1,)), ((), ())), preferred_element_type=F32)
            q2[base : base + slab, :] = (t * key_scale).astype(BF16)

        state = {}

        def attend_rows(base, n, m, l, first, count):
            at = slice(base, base + n)
            keys = kv[first : first + count].reshape(count * 2 * slab, width)
            s = lax.dot_general(
                q2[at, :], keys, (((1,), (1,)), ((), ())), preferred_element_type=F32
            )
            top = jnp.max(s, axis=-1, keepdims=True)
            if m is not None:
                top = jnp.maximum(m, top)
                alpha = jnp.exp2(m - top)
            p = jnp.exp2(s - top).astype(BF16)
            psum = jnp.sum(p.astype(F32), axis=-1, keepdims=True)
            o = jnp.dot(p, keys, preferred_element_type=F32)
            if m is not None:
                psum = l * alpha + psum
                o = acc[at, :] * alpha + o
            acc[at, :] = o
            return top, psum

        def attend(who, first, count):
            m, l = state.get(who, (None, None))
            state[who] = attend_rows(who * slab, slab, m, l, first, count)

        def finished(base, n, m, l):
            mean_key = acc[base : base + n, :] / l
            return (mean_key * scale1 + base1).astype(BF16), m + jnp.log(l) * LOG2E

        diag = lax.broadcasted_iota(jnp.int32, (slab, width), 0) == lax.broadcasted_iota(
            jnp.int32, (slab, width), 1
        )

        OWN, OTHER = 0, 1
        make_queries(own, 0)
        pass_on(6, 7)
        to_partner.wait_recv()
        make_queries(xq[...].astype(F32), slab)
        pass_on(7, 8)
        start(sibs[3:5])
        mates(0)
        attend(OTHER, 0, 1)
        mates(1)
        attend(OTHER, 1, 2)
        pass_on(8, 9)
        mates(2)
        attend(OTHER, 3, 2)
        pass_on(9, 10)
        attend(OWN, 0, 1)
        pass_on(10, 11)
        attend(OWN, 1, 2)
        pass_on(11, 12)
        start(sibs[5:7])
        attend(OWN, 3, 2)
        pass_on(12, 13)
        mates(3)
        attend(OTHER, 5, 2)
        pass_on(13, 14)
        sibs[7].start()
        mates(4)
        halfway = slab // 2
        halves = [slice(0, halfway), slice(halfway, slab)]
        part_copies = [
            send(part.at[pl.ds(i * halfway, halfway)], partin.at[pl.ds(i * halfway, halfway)], tail_s, misc_r.at[1 + i], partner)
            for i in range(2)
        ]
        lse_copy = send(lse, lsein, lse_s, misc_r.at[3], partner)
        m, l = state[OTHER]
        weights = []
        for i, at in enumerate(halves):
            top, total_l = attend_rows(slab + i * halfway, halfway, m[at], l[at], 7, 1)
            part[at, :], w = finished(slab + i * halfway, halfway, top, total_l)
            weights.append(w)
            if i == 1:
                w = jnp.concatenate(weights, axis=0)
                lse[...] = jnp.sum(jnp.where(diag, w, 0.0), axis=0, keepdims=True)
                lse_copy.start()
            part_copies[i].start()
        attend(OWN, 5, 2)
        attend(OWN, 7, 1)
        o1, w1 = finished(0, slab, *state[OWN])
        y1 = jnp.dot(o1, w4[2], preferred_element_type=F32)
        base = kv[0, 0:slab].astype(F32) + vrow(2)
        lse_copy.wait_recv()
        w2 = jnp.sum(jnp.where(diag, lsein[...], 0.0), axis=1, keepdims=True)
        top = jnp.maximum(w1, w2)
        e1 = jnp.exp2(w1 - top)
        e2 = jnp.exp2(w2 - top)
        inv = 1.0 / (e1 + e2)
        base = base + y1 * (e1 * inv)
        e2 = e2 * inv
        mixed = []
        for i, at in enumerate(halves):
            part_copies[i].wait_recv()
            y2 = jnp.dot(partin[at, :], w4[2], preferred_element_type=F32)
            mixed.append((base[at] + y2 * e2[at]).astype(BF16))
        mixed = jnp.concatenate(mixed, axis=0)
        curm[0:slab, :] = mixed
        top_row = pl.ds(0, cols)
        low_row = pl.ds(slab, cols)
        bottom_row = pl.ds(cols, slab - cols)
        halos = [
            send(curm.at[top_row], earm.at[top_row], tail_s, misc_r.at[4], (later, h)),
            send(curm.at[bottom_row], earm.at[bottom_row], tail_s, misc_r.at[5], (later, h)),
            send(curm.at[top_row], curm.at[low_row], tail_s, misc_r.at[6], (f, above)),
            send(earm.at[top_row], earm.at[low_row], tail_s, misc_r.at[7], (f, above)),
        ]
        local_stats(mixed.astype(F32), 2)
        start(far2)
        start(halos[:3])
        told(2)
        merge_to(2, 3, float(slab))
        start(near2)
        halos[0].wait_recv()
        halos[3].start()
        told(3)
        mean2, rstd2 = group_stats(3)
        scale2 = vrow(3) * rstd2
        shift2 = vrow(4)

        last_col = lax.broadcasted_iota(jnp.int32, (cols, width), 0) == cols - 1

        def activate(src, which, r, keep):
            x = src[r * cols : (r + 1) * cols, :].astype(F32)
            v = (x - mean2) * scale2 + shift2
            y = v / (1.0 + jnp.exp(-v))
            if keep is not None:
                y = jnp.where(keep, y, 0.0)
            act[which, 0, r * cols : (r + 1) * cols, :] = y.astype(BF16)
            y = jnp.where(last_col, 0.0, pltpu.roll(y, cols - 1, 0))
            act[which, 1, r * cols : (r + 1) * cols, :] = y.astype(BF16)

        has_below = h < nh - 1
        has_sooner = f > 0
        for r in range(rows):
            activate(curm, 0, r, None)
        for copy in halos[1:]:
            copy.wait_recv()
        activate(curm, 0, rows, has_below)
        for r in range(rows):
            activate(earm, 1, r, has_sooner)
        activate(earm, 1, rows, jnp.logical_and(has_below, has_sooner))
        up_copy.wait()

        taps = (((0, 1),), ((0, 2), (1, 0)))
        for b in range(2):
            for c in range(2):
                wins = [(rs, cs, q, r) for rs, q in taps[b] for cs, r in taps[c]]

                def windows(which):
                    parts = [act[which, cs, rs * cols : rs * cols + slab, :] for rs, cs, _, _ in wins]
                    return parts[0] if len(parts) == 1 else jnp.concatenate(parts, axis=1)

                def weights(p):
                    parts = [wupv[p, q, r] for _, _, q, r in wins]
                    return parts[0] if len(parts) == 1 else jnp.concatenate(parts, axis=0)

                current = windows(0)
                both = jnp.dot(
                    current,
                    jnp.concatenate([weights(0), weights(1)], axis=1),
                    preferred_element_type=F32,
                )
                y0 = both[:, 0:width] + jnp.dot(windows(1), weights(2), preferred_element_type=F32)
                for a, y in ((0, y0), (1, both[:, width:])):
                    y = y + vrow(5)
                    for i in range(rows):
                        for n in range(lanes):
                            stage[a, i, n, pl.ds(c, cols, stride=2), :] = y[
                                i * cols : (i + 1) * cols, n * 128 : (n + 1) * 128
                            ]
            for a in range(2):
                for i in range(rows):
                    for n in range(lanes):
                        out[a, 2 * i + b, :, n * 128 : (n + 1) * 128] = stage[a, i, n].astype(BF16)

        took(kv_s, kv)
        took(tail_s, act.at[0])
        lse_copy.wait_send()
        for slot in range(4):
            took(st_s.at[slot], st.at[slot, pl.ds(1, group - 1)])

    slab2 = 2 * slab
    dma = pltpu.SemaphoreType.DMA
    scratch = [
        pltpu.VMEM((NSLOT, slab2, width), BF16),
        pltpu.VMEM((slab, width), BF16),
        pltpu.VMEM((slab2, width), BF16),
        pltpu.VMEM((slab2, width), F32),
        pltpu.VMEM((slab, width), BF16),
        pltpu.VMEM((slab, width), BF16),
        pltpu.VMEM((1, width), F32),
        pltpu.VMEM((1, width), F32),
        pltpu.VMEM((4, width, width), BF16),
        pltpu.VMEM((3, 3, 3, width, width), BF16),
        *[pltpu.VMEM((width,), F32)] * 6,
        pltpu.VMEM((width, width), BF16),
        pltpu.VMEM((4, group, 1, 2 * width), F32),
        pltpu.VMEM((slab + cols, width), BF16),
        pltpu.VMEM((slab + cols, width), BF16),
        pltpu.VMEM((2, 2, slab + cols, width), BF16),
        pltpu.VMEM((2, rows, lanes, 2 * cols, 128), F32),
        dma((4,)),
        dma((4,)),
        dma,
        dma((steps,)),
        dma((5,)),
        dma,
        dma((8,)),
        dma,
        dma((3,)),
        dma((6,)),
    ]
    return kernel, scratch


def solution(mesh):
    nf, nh = mesh.shape["frames"], mesh.shape["height"]

    def local(
        latent, first_gain, first_shift, query_weight, key_weight, value_weight, out_weight, out_bias,
        second_gain, second_shift, up_weight, up_bias,
    ):
        _, rows, cols, width = latent.shape
        kernel, scratch = make_kernel(nf, nh, rows, cols, width)

        out = pl.pallas_call(
            kernel,
            out_shape=pltpu.VMEM((2, 2 * rows, 2 * cols, width), BF16),
            in_specs=[pl.BlockSpec(memory_space=pl.ANY)] * 12,
            out_specs=pl.BlockSpec(memory_space=pltpu.VMEM),
            scratch_shapes=scratch,
            compiler_params=pltpu.CompilerParams(
                collective_id=0, has_side_effects=True, vmem_limit_bytes=56 * 1024 * 1024
            ),
            name="decoder_window",
        )(
            latent.reshape(rows * cols, width),
            first_gain, first_shift,
            query_weight, key_weight, value_weight, out_weight,
            out_bias, second_gain, second_shift,
            up_weight, up_bias,
        )
        return out

    whole = P("frames", "height", None, None)
    return jax.shard_map(
        local, mesh=mesh, in_specs=(whole,) + (P(),) * 11, out_specs=whole, check_vma=False
    )
```

```python
import jax
import jax.numpy as jnp
from jax import lax
from jax.experimental import pallas as pl
from jax.experimental.pallas import tpu as pltpu
from jax.sharding import PartitionSpec as P

GROUPS = 32
EPS = 1e-05
LOG2E = 1.4426950408889634
MESH = pl.DeviceIdType.MESH
BF16 = jnp.bfloat16
F32 = jnp.float32

NSLOT = 8
PIECES = 4


def make_kernel(nf, nh, rows, cols, width):
    slab = rows * cols
    piece = slab // PIECES
    steps = 3 * PIECES + PIECES // 2
    group = 16
    nx = nh // group
    total = float(nf * nh * slab)
    per_group = width // GROUPS
    lanes = width // 128

    def kernel(
        lat, g1, s1, wq, wk, wv, wo, ob, g2, s2, wup, ub, out,
        kv, xq, q2, acc, part, partin, lse, lsein, w4, wupv,
        g1v, s1v, obv, g2v, s2v, ubv, same, member,
        st, curm, earm, act, stage,
        st_s, st_r, kv_s, ring_r, sib_r, tail_s, misc_r, lse_s, loc, locv,
    ):
        vec = (g1v, s1v, obv, g2v, s2v, ubv)
        f = lax.axis_index("frames")
        h = lax.axis_index("height")
        xh = h // group
        k = h % group
        e = f * nx + xh

        def near(j):
            return (f, xh * group + (k + j) % group)

        def far(j):
            other = (e + j) % group
            return (other // nx, (other % nx) * group + k)

        right = near(2)
        left = near(group - 2)
        sibling = (f, xh * group + k + 1 - 2 * (k % 2))
        partner = (f, (h + group) % nh)
        above = (h + nh - 1) % nh
        below = (h + 1) % nh
        later = (f + 1) % nf

        def vrow(i):
            return vec[i][...].reshape(1, width)

        barrier = pltpu.get_barrier_semaphore()

        def greet(dev):
            pl.semaphore_signal(barrier, inc=1, device_id=dev, device_id_type=MESH)

        own_copy = pltpu.make_async_copy(lat, kv.at[0, pl.ds(0, slab)], loc.at[0])
        own_copy.start()

        def greet_both(j, carry):
            greet(near(j))
            greet(far(j))
            return carry

        lax.fori_loop(1, group, greet_both, 0)
        for dev in ((f, above), (f, below)):
            greet(dev)

        small = [
            pltpu.make_async_copy(src, w4.at[i], loc.at[1]) for i, src in enumerate((wq, wk, wv, wo))
        ]
        rows_in = [
            pltpu.make_async_copy(src, dst, locv.at[i])
            for i, (src, dst) in enumerate(zip((g1, s1, ob, g2, s2, ub), vec))
        ]
        for copy in small + rows_in:
            copy.start()
        up_copy = pltpu.make_async_copy(wup, wupv, loc.at[2])

        def send(src, dst, ss, rs, dev):
            return pltpu.make_async_remote_copy(
                src_ref=src, dst_ref=dst, send_sem=ss, recv_sem=rs, device_id=dev, device_id_type=MESH
            )

        def took(sem, size):
            pltpu.make_async_copy(size, size, sem).wait()

        def ring(step, to_right):
            hop = step // PIECES
            source = 0 if hop == 0 else (2 * hop - 1 if to_right else 2 * hop)
            target = 7 if hop == 3 else (2 * hop + 1 if to_right else 2 * hop + 2)
            at = pl.ds(((step % PIECES) + (0 if hop < 3 or to_right else PIECES // 2)) * piece, piece)
            return send(
                kv.at[source, at], kv.at[target, at], kv_s, ring_r.at[step], right if to_right else left
            )

        rings = {(s, d): ring(s, d) for s in range(steps) for d in (True, False)}

        def pass_on(first, last):
            for s in range(first * PIECES // 4, last * PIECES // 4):
                took(ring_r.at[s], kv.at[0, pl.ds(0, 2 * piece)])
                for d in (True, False):
                    onward = s + PIECES
                    if onward >= 3 * PIECES and not d:
                        onward -= PIECES // 2
                        if onward < 3 * PIECES:
                            continue
                    if onward < steps:
                        rings[onward, d].start()

        sibs = [
            send(kv.at[s, pl.ds(0, slab)], kv.at[s, pl.ds(slab, slab)], kv_s, sib_r.at[(s + 1) // 2], sibling)
            for s in range(NSLOT)
        ]
        to_partner = send(kv.at[0, pl.ds(0, slab)], xq, kv_s, misc_r.at[0], partner)

        line = lax.broadcasted_iota(jnp.int32, (16, width), 0)

        def pieces_of(row, first):
            high = row.astype(BF16).astype(F32)
            rest = row - high
            middle = rest.astype(BF16).astype(F32)
            at = line[:, 0 : row.shape[1]] - first
            rows_ = jnp.where(at == 0, high, jnp.where(at == 1, middle, rest - middle))
            return jnp.where((at >= 0) & (at < 3), rows_, 0.0)

        def sums(pieces, matrix):
            return jnp.dot(pieces.astype(BF16), matrix, preferred_element_type=F32)

        def local_stats(x, slot):
            mean = jnp.sum(x, axis=0, keepdims=True) * (1.0 / slab)
            pieces = pieces_of(mean, 0)
            spread = jnp.sum(sums(pieces, same[...]), axis=0, keepdims=True) * (1.0 / per_group)
            gmean = jnp.sum(sums(pieces, member[...]), axis=0, keepdims=True) * (1.0 / per_group)
            d = x - mean
            apart = mean - spread
            m2 = jnp.sum(d * d, axis=0, keepdims=True) + float(slab) * apart * apart
            m2 = jnp.sum(sums(pieces_of(m2, 0), member[...]), axis=0, keepdims=True)
            st[slot, 0] = jnp.concatenate([gmean, m2], axis=1)

        def messages(slot, peer):
            return [
                send(st.at[slot, 0], st.at[slot, j], st_s.at[slot], st_r.at[slot], peer(j))
                for j in sorted(range(1, group), key=lambda j: abs(j - group // 2))
            ]

        def start(copies):
            for copy in copies:
                copy.start()

        def told(slot):
            took(st_r.at[slot], st.at[slot, pl.ds(1, group - 1)])

        def mates(i):
            took(sib_r.at[i], kv.at[0] if 0 < i < 4 else kv.at[0, pl.ds(0, slab)])

        def merged(slot, devices):
            means = [st[slot, j, :, 0:128] for j in range(group)]
            mean = sum(means) * (1.0 / group)
            m2 = sum(st[slot, j, :, 128:256] for j in range(group))
            count = float(devices * slab * per_group)
            return mean, m2 + count * sum((one - mean) * (one - mean) for one in means)

        def merge_to(slot, target):
            mean, m2 = merged(slot, 1)
            st[target, 0] = jnp.concatenate([mean, m2], axis=1)

        def group_stats(slot):
            gmean, m2 = merged(slot, group)
            grstd = lax.rsqrt(m2 * (1.0 / (per_group * total)) + EPS)
            pieces = pieces_of(gmean, 0) + pieces_of(grstd, 8)
            wide = lax.dot_general(
                pieces.astype(BF16), member[...], (((1,), (1,)), ((), ())), preferred_element_type=F32
            )
            return (
                jnp.sum(wide[0:8], axis=0, keepdims=True),
                jnp.sum(wide[8:16], axis=0, keepdims=True),
            )

        near1, far1 = messages(0, near), messages(1, far)
        far2, near2 = messages(2, far), messages(3, near)

        own_copy.wait()
        own = kv[0, 0:slab].astype(F32)
        grp_row = (lax.broadcasted_iota(jnp.int32, (width, width), 0) * 5462) >> 16
        grp_col = (lax.broadcasted_iota(jnp.int32, (width, width), 1) * 5462) >> 16
        same[...] = jnp.where(grp_row == grp_col, 1.0, 0.0).astype(BF16)
        grp_lane = lax.broadcasted_iota(jnp.int32, (width, 128), 1)
        member[...] = jnp.where(grp_row[:, 0:128] == grp_lane, 1.0, 0.0).astype(BF16)
        local_stats(own, 0)
        pl.semaphore_wait(barrier, 2 * (group - 1) + 2)
        start(near1)
        for s in range(PIECES):
            rings[s, True].start()
            rings[s, False].start()
        to_partner.start()
        sibs[0].start()
        up_copy.start()
        took(loc.at[1], w4)
        for copy in rows_in:
            copy.wait()
        value_out = jnp.dot(w4[2], w4[3], preferred_element_type=F32).astype(BF16)
        w4[2] = value_out
        told(0)
        merge_to(0, 1)
        start(far1)
        pass_on(0, 4)
        start(sibs[1:3])
        pass_on(4, 5)
        told(1)
        mean1, rstd1 = group_stats(1)
        pass_on(5, 6)
        scale1 = vrow(0) * rstd1
        shift1 = vrow(1)
        base1 = shift1 - mean1 * scale1
        key_scale = scale1 * (width**-0.5 * LOG2E)

        def make_queries(x, base):
            normed = ((x - mean1) * scale1 + shift1).astype(BF16)
            q = jnp.dot(normed, w4[0], preferred_element_type=F32).astype(BF16)
            t = lax.dot_general(q, w4[1], (((1,), (1,)), ((), ())), preferred_element_type=F32)
            q2[base : base + slab, :] = (t * key_scale).astype(BF16)

        state = {}

        def attend_rows(base, n, m, l, first, count):
            at = slice(base, base + n)
            keys = kv[first : first + count].reshape(count * 2 * slab, width)
            s = lax.dot_general(
                q2[at, :], keys, (((1,), (1,)), ((), ())), preferred_element_type=F32
            )
            top = jnp.max(s, axis=-1, keepdims=True)
            if m is not None:
                top = jnp.maximum(m, top)
                alpha = jnp.exp2(m - top)
            p = jnp.exp2(s - top).astype(BF16)
            psum = jnp.sum(p.astype(F32), axis=-1, keepdims=True)
            o = jnp.dot(p, keys, preferred_element_type=F32)
            if m is not None:
                psum = l * alpha + psum
                o = acc[at, :] * alpha + o
            acc[at, :] = o
            return top, psum

        def attend(who, first, count):
            m, l = state.get(who, (None, None))
            state[who] = attend_rows(who * slab, slab, m, l, first, count)

        def finished(base, n, m, l):
            mean_key = acc[base : base + n, :] / l
            return (mean_key * scale1 + base1).astype(BF16), m + jnp.log(l) * LOG2E

        diag = lax.broadcasted_iota(jnp.int32, (slab, width), 0) == lax.broadcasted_iota(
            jnp.int32, (slab, width), 1
        )

        OWN, OTHER = 0, 1
        make_queries(own, 0)
        pass_on(6, 7)
        to_partner.wait_recv()
        make_queries(xq[...].astype(F32), slab)
        pass_on(7, 8)
        start(sibs[3:5])
        mates(0)
        attend(OTHER, 0, 1)
        mates(1)
        attend(OTHER, 1, 2)
        pass_on(8, 9)
        mates(2)
        attend(OTHER, 3, 2)
        pass_on(9, 10)
        attend(OWN, 0, 1)
        pass_on(10, 11)
        attend(OWN, 1, 2)
        pass_on(11, 12)
        start(sibs[5:7])
        attend(OWN, 3, 2)
        pass_on(12, 13)
        mates(3)
        attend(OTHER, 5, 2)
        pass_on(13, 14)
        sibs[7].start()
        mates(4)
        halfway = slab // 2
        halves = [slice(0, halfway), slice(halfway, slab)]
        part_copies = [
            send(part.at[pl.ds(i * halfway, halfway)], partin.at[pl.ds(i * halfway, halfway)], tail_s, misc_r.at[1 + i], partner)
            for i in range(2)
        ]
        lse_copy = send(lse, lsein, lse_s, misc_r.at[3], partner)
        m, l = state[OTHER]
        weights = []
        for i, at in enumerate(halves):
            top, total_l = attend_rows(slab + i * halfway, halfway, m[at], l[at], 7, 1)
            part[at, :], w = finished(slab + i * halfway, halfway, top, total_l)
            weights.append(w)
            if i == 1:
                w = jnp.concatenate(weights, axis=0)
                lse[...] = jnp.sum(jnp.where(diag, w, 0.0), axis=0, keepdims=True)
                lse_copy.start()
            part_copies[i].start()
        attend(OWN, 5, 2)
        attend(OWN, 7, 1)
        o1, w1 = finished(0, slab, *state[OWN])
        y1 = jnp.dot(o1, w4[2], preferred_element_type=F32)
        base = kv[0, 0:slab].astype(F32) + vrow(2)
        lse_copy.wait_recv()
        w2 = jnp.sum(jnp.where(diag, lsein[...], 0.0), axis=1, keepdims=True)
        top = jnp.maximum(w1, w2)
        e1 = jnp.exp2(w1 - top)
        e2 = jnp.exp2(w2 - top)
        inv = 1.0 / (e1 + e2)
        base = base + y1 * (e1 * inv)
        e2 = e2 * inv
        mixed = []
        for i, at in enumerate(halves):
            part_copies[i].wait_recv()
            y2 = jnp.dot(partin[at, :], w4[2], preferred_element_type=F32)
            mixed.append((base[at] + y2 * e2[at]).astype(BF16))
        mixed = jnp.concatenate(mixed, axis=0)
        curm[0:slab, :] = mixed
        top_row = pl.ds(0, cols)
        low_row = pl.ds(slab, cols)
        bottom_row = pl.ds(cols, slab - cols)
        halos = [
            send(curm.at[top_row], earm.at[top_row], tail_s, misc_r.at[4], (later, h)),
            send(curm.at[bottom_row], earm.at[bottom_row], tail_s, misc_r.at[5], (later, h)),
            send(curm.at[top_row], curm.at[low_row], tail_s, misc_r.at[6], (f, above)),
            send(earm.at[top_row], earm.at[low_row], tail_s, misc_r.at[7], (f, above)),
        ]
        local_stats(mixed.astype(F32), 2)
        start(far2)
        start(halos[:3])
        told(2)
        merge_to(2, 3)
        start(near2)
        halos[0].wait_recv()
        halos[3].start()
        told(3)
        mean2, rstd2 = group_stats(3)
        scale2 = vrow(3) * rstd2
        shift2 = vrow(4)

        last_col = lax.broadcasted_iota(jnp.int32, (cols, width), 0) == cols - 1

        def activate(src, which, r, keep):
            x = src[r * cols : (r + 1) * cols, :].astype(F32)
            v = (x - mean2) * scale2 + shift2
            y = v / (1.0 + jnp.exp(-v))
            if keep is not None:
                y = jnp.where(keep, y, 0.0)
            act[which, 0, r * cols : (r + 1) * cols, :] = y.astype(BF16)
            y = jnp.where(last_col, 0.0, pltpu.roll(y, cols - 1, 0))
            act[which, 1, r * cols : (r + 1) * cols, :] = y.astype(BF16)

        has_below = h < nh - 1
        has_sooner = f > 0
        for r in range(rows):
            activate(curm, 0, r, None)
        for copy in halos[1:]:
            copy.wait_recv()
        activate(curm, 0, rows, has_below)
        for r in range(rows):
            activate(earm, 1, r, has_sooner)
        activate(earm, 1, rows, jnp.logical_and(has_below, has_sooner))
        up_copy.wait()

        taps = (((0, 1),), ((0, 2), (1, 0)))
        for b in range(2):
            for c in range(2):
                wins = [(rs, cs, q, r) for rs, q in taps[b] for cs, r in taps[c]]

                def windows(which):
                    parts = [act[which, cs, rs * cols : rs * cols + slab, :] for rs, cs, _, _ in wins]
                    return parts[0] if len(parts) == 1 else jnp.concatenate(parts, axis=1)

                def weights(p):
                    parts = [wupv[p, q, r] for _, _, q, r in wins]
                    return parts[0] if len(parts) == 1 else jnp.concatenate(parts, axis=0)

                current = windows(0)
                both = jnp.dot(
                    current,
                    jnp.concatenate([weights(0), weights(1)], axis=1),
                    preferred_element_type=F32,
                )
                y0 = both[:, 0:width] + jnp.dot(windows(1), weights(2), preferred_element_type=F32)
                for a, y in ((0, y0), (1, both[:, width:])):
                    y = y + vrow(5)
                    for i in range(rows):
                        for n in range(lanes):
                            stage[a, i, n, pl.ds(c, cols, stride=2), :] = y[
                                i * cols : (i + 1) * cols, n * 128 : (n + 1) * 128
                            ]
            for a in range(2):
                for i in range(rows):
                    for n in range(lanes):
                        out[a, 2 * i + b, :, n * 128 : (n + 1) * 128] = stage[a, i, n].astype(BF16)

        took(kv_s, kv)
        took(tail_s, act.at[0])
        lse_copy.wait_send()
        for slot in range(4):
            took(st_s.at[slot], st.at[slot, pl.ds(1, group - 1)])

    slab2 = 2 * slab
    dma = pltpu.SemaphoreType.DMA
    scratch = [
        pltpu.VMEM((NSLOT, slab2, width), BF16),
        pltpu.VMEM((slab, width), BF16),
        pltpu.VMEM((slab2, width), BF16),
        pltpu.VMEM((slab2, width), F32),
        pltpu.VMEM((slab, width), BF16),
        pltpu.VMEM((slab, width), BF16),
        pltpu.VMEM((1, width), F32),
        pltpu.VMEM((1, width), F32),
        pltpu.VMEM((4, width, width), BF16),
        pltpu.VMEM((3, 3, 3, width, width), BF16),
        *[pltpu.VMEM((width,), F32)] * 6,
        pltpu.VMEM((width, width), BF16),
        pltpu.VMEM((width, 128), BF16),
        pltpu.VMEM((4, group, 1, 256), F32),
        pltpu.VMEM((slab + cols, width), BF16),
        pltpu.VMEM((slab + cols, width), BF16),
        pltpu.VMEM((2, 2, slab + cols, width), BF16),
        pltpu.VMEM((2, rows, lanes, 2 * cols, 128), F32),
        dma((4,)),
        dma((4,)),
        dma,
        dma((steps,)),
        dma((5,)),
        dma,
        dma((8,)),
        dma,
        dma((3,)),
        dma((6,)),
    ]
    return kernel, scratch


def solution(mesh):
    nf, nh = mesh.shape["frames"], mesh.shape["height"]

    def local(
        latent, first_gain, first_shift, query_weight, key_weight, value_weight, out_weight, out_bias,
        second_gain, second_shift, up_weight, up_bias,
    ):
        _, rows, cols, width = latent.shape
        kernel, scratch = make_kernel(nf, nh, rows, cols, width)

        out = pl.pallas_call(
            kernel,
            out_shape=pltpu.VMEM((2, 2 * rows, 2 * cols, width), BF16),
            in_specs=[pl.BlockSpec(memory_space=pl.ANY)] * 12,
            out_specs=pl.BlockSpec(memory_space=pltpu.VMEM),
            scratch_shapes=scratch,
            compiler_params=pltpu.CompilerParams(
                collective_id=0, has_side_effects=True, vmem_limit_bytes=56 * 1024 * 1024
            ),
            name="decoder_window",
        )(
            latent.reshape(rows * cols, width),
            first_gain, first_shift,
            query_weight, key_weight, value_weight, out_weight,
            out_bias, second_gain, second_shift,
            up_weight, up_bias,
        )
        return out

    whole = P("frames", "height", None, None)
    return jax.shard_map(
        local, mesh=mesh, in_specs=(whole,) + (P(),) * 11, out_specs=whole, check_vma=False
    )
```

```python
import jax
import jax.numpy as jnp
from jax import lax
from jax.experimental import pallas as pl
from jax.experimental.pallas import tpu as pltpu
from jax.sharding import PartitionSpec as P

GROUPS = 32
EPS = 1e-05
LOG2E = 1.4426950408889634
MESH = pl.DeviceIdType.MESH
BF16 = jnp.bfloat16
F32 = jnp.float32

NSLOT = 8
PIECES = 4


def make_kernel(nf, nh, rows, cols, width):
    slab = rows * cols
    piece = slab // PIECES
    steps = 3 * PIECES + PIECES // 2
    group = 16
    nx = nh // group
    total = float(nf * nh * slab)
    per_group = width // GROUPS
    lanes = width // 128

    def kernel(
        lat, g1, s1, wq, wk, wv, wo, ob, g2, s2, wup, ub, out,
        kv, xq, q2, acc, part, partin, lse, lsein, w4, wupv,
        g1v, s1v, obv, g2v, s2v, ubv, same, member,
        st, curm, earm, act, stage,
        st_s, st_r, kv_s, ring_r, sib_r, tail_s, misc_r, lse_s, loc, locv,
    ):
        vec = (g1v, s1v, obv, g2v, s2v, ubv)
        f = lax.axis_index("frames")
        h = lax.axis_index("height")
        xh = h // group
        k = h % group
        e = f * nx + xh

        def near(j):
            return (f, xh * group + (k + j) % group)

        def far(j):
            other = (e + j) % group
            return (other // nx, (other % nx) * group + k)

        right = near(2)
        left = near(group - 2)
        sibling = (f, xh * group + k + 1 - 2 * (k % 2))
        partner = (f, (h + group) % nh)
        above = (h + nh - 1) % nh
        below = (h + 1) % nh
        later = (f + 1) % nf

        def vrow(i):
            return vec[i][...].reshape(1, width)

        barrier = pltpu.get_barrier_semaphore()

        def greet(dev):
            pl.semaphore_signal(barrier, inc=1, device_id=dev, device_id_type=MESH)

        own_copy = pltpu.make_async_copy(lat, kv.at[0, pl.ds(0, slab)], loc.at[0])
        own_copy.start()

        def greet_both(j, carry):
            greet(near(j))
            greet(far(j))
            return carry

        lax.fori_loop(1, group, greet_both, 0)
        for dev in ((f, above), (f, below)):
            greet(dev)

        small = [
            pltpu.make_async_copy(src, w4.at[i], loc.at[1]) for i, src in enumerate((wq, wk, wv, wo))
        ]
        rows_in = [
            pltpu.make_async_copy(src, dst, locv.at[i])
            for i, (src, dst) in enumerate(zip((g1, s1, ob, g2, s2, ub), vec))
        ]
        for copy in small + rows_in:
            copy.start()
        up_copy = pltpu.make_async_copy(wup, wupv, loc.at[2])

        def send(src, dst, ss, rs, dev):
            return pltpu.make_async_remote_copy(
                src_ref=src, dst_ref=dst, send_sem=ss, recv_sem=rs, device_id=dev, device_id_type=MESH
            )

        def took(sem, size):
            pltpu.make_async_copy(size, size, sem).wait()

        def ring(step, to_right):
            hop = step // PIECES
            source = 0 if hop == 0 else (2 * hop - 1 if to_right else 2 * hop)
            target = 7 if hop == 3 else (2 * hop + 1 if to_right else 2 * hop + 2)
            at = pl.ds(((step % PIECES) + (0 if hop < 3 or to_right else PIECES // 2)) * piece, piece)
            return send(
                kv.at[source, at], kv.at[target, at], kv_s, ring_r.at[step], right if to_right else left
            )

        rings = {(s, d): ring(s, d) for s in range(steps) for d in (True, False)}

        def pass_on(first, last):
            for s in range(first * PIECES // 4, last * PIECES // 4):
                took(ring_r.at[s], kv.at[0, pl.ds(0, 2 * piece)])
                for d in (True, False):
                    onward = s + PIECES
                    if onward >= 3 * PIECES and not d:
                        onward -= PIECES // 2
                        if onward < 3 * PIECES:
                            continue
                    if onward < steps:
                        rings[onward, d].start()

        sibs = [
            send(kv.at[s, pl.ds(0, slab)], kv.at[s, pl.ds(slab, slab)], kv_s, sib_r.at[(s + 1) // 2], sibling)
            for s in range(NSLOT)
        ]
        to_partner = send(kv.at[0, pl.ds(0, slab)], xq, kv_s, misc_r.at[0], partner)

        line = lax.broadcasted_iota(jnp.int32, (16, width), 0)

        def pieces_of(row, first):
            high = row.astype(BF16).astype(F32)
            rest = row - high
            middle = rest.astype(BF16).astype(F32)
            at = line[:, 0 : row.shape[1]] - first
            rows_ = jnp.where(at == 0, high, jnp.where(at == 1, middle, rest - middle))
            return jnp.where((at >= 0) & (at < 3), rows_, 0.0)

        def sums(pieces, matrix):
            return jnp.dot(pieces.astype(BF16), matrix, preferred_element_type=F32)

        def local_stats(x, slot):
            mean = jnp.sum(x, axis=0, keepdims=True) * (1.0 / slab)
            pieces = pieces_of(mean, 0)
            spread = jnp.sum(sums(pieces, same[...]), axis=0, keepdims=True) * (1.0 / per_group)
            gmean = jnp.sum(sums(pieces, member[...]), axis=0, keepdims=True) * (1.0 / per_group)
            d = x - mean
            apart = mean - spread
            m2 = jnp.sum(d * d, axis=0, keepdims=True) + float(slab) * apart * apart
            m2 = jnp.sum(sums(pieces_of(m2, 0), member[...]), axis=0, keepdims=True)
            st[slot, 0] = jnp.concatenate([gmean, m2], axis=1)

        def messages(slot, peer):
            return [
                send(st.at[slot, 0], st.at[slot, j], st_s.at[slot], st_r.at[slot], peer(j))
                for j in sorted(range(1, group), key=lambda j: abs(j - group // 2))
            ]

        def start(copies):
            for copy in copies:
                copy.start()

        def told(slot):
            took(st_r.at[slot], st.at[slot, pl.ds(1, group - 1)])

        def mates(i):
            took(sib_r.at[i], kv.at[0] if 0 < i < 4 else kv.at[0, pl.ds(0, slab)])

        def merged(slot, devices):
            means = [st[slot, j, :, 0:128] for j in range(group)]
            mean = sum(means) * (1.0 / group)
            m2 = sum(st[slot, j, :, 128:256] for j in range(group))
            count = float(devices * slab * per_group)
            return mean, m2 + count * sum((one - mean) * (one - mean) for one in means)

        def merge_to(slot, target):
            mean, m2 = merged(slot, 1)
            st[target, 0] = jnp.concatenate([mean, m2], axis=1)

        def group_stats(slot):
            gmean, m2 = merged(slot, group)
            grstd = lax.rsqrt(m2 * (1.0 / (per_group * total)) + EPS)
            pieces = pieces_of(gmean, 0) + pieces_of(grstd, 8)
            wide = lax.dot_general(
                pieces.astype(BF16), member[...], (((1,), (1,)), ((), ())), preferred_element_type=F32
            )
            return (
                jnp.sum(wide[0:8], axis=0, keepdims=True),
                jnp.sum(wide[8:16], axis=0, keepdims=True),
            )

        near1, far1 = messages(0, near), messages(1, far)
        far2, near2 = messages(2, far), messages(3, near)

        own_copy.wait()
        own = kv[0, 0:slab].astype(F32)
        grp_row = (lax.broadcasted_iota(jnp.int32, (width, width), 0) * 5462) >> 16
        grp_col = (lax.broadcasted_iota(jnp.int32, (width, width), 1) * 5462) >> 16
        same[...] = jnp.where(grp_row == grp_col, 1.0, 0.0).astype(BF16)
        grp_lane = lax.broadcasted_iota(jnp.int32, (width, 128), 1)
        member[...] = jnp.where(grp_row[:, 0:128] == grp_lane, 1.0, 0.0).astype(BF16)
        local_stats(own, 0)
        pl.semaphore_wait(barrier, 2 * (group - 1) + 2)
        start(near1)
        for s in range(PIECES):
            rings[s, True].start()
            rings[s, False].start()
        to_partner.start()
        sibs[0].start()
        up_copy.start()
        took(loc.at[1], w4)
        for copy in rows_in:
            copy.wait()
        value_out = jnp.dot(w4[2], w4[3], preferred_element_type=F32).astype(BF16)
        w4[2] = value_out
        told(0)
        merge_to(0, 1)
        start(far1)
        pass_on(0, 4)
        start(sibs[1:3])
        pass_on(4, 5)
        told(1)
        mean1, rstd1 = group_stats(1)
        pass_on(5, 6)
        scale1 = vrow(0) * rstd1
        shift1 = vrow(1)
        base1 = shift1 - mean1 * scale1
        key_scale = scale1 * (width**-0.5 * LOG2E)

        def make_queries(x, base):
            normed = ((x - mean1) * scale1 + shift1).astype(BF16)
            q = jnp.dot(normed, w4[0], preferred_element_type=F32).astype(BF16)
            t = lax.dot_general(q, w4[1], (((1,), (1,)), ((), ())), preferred_element_type=F32)
            q2[base : base + slab, :] = (t * key_scale).astype(BF16)

        state = {}

        def attend_rows(base, n, m, l, first, count):
            at = slice(base, base + n)
            keys = kv[first : first + count].reshape(count * 2 * slab, width)
            s = lax.dot_general(
                q2[at, :], keys, (((1,), (1,)), ((), ())), preferred_element_type=F32
            )
            top = jnp.max(s, axis=-1, keepdims=True)
            if m is not None:
                top = jnp.maximum(m, top)
                alpha = jnp.exp2(m - top)
            p = jnp.exp2(s - top).astype(BF16)
            psum = jnp.sum(p.astype(F32), axis=-1, keepdims=True)
            o = jnp.dot(p, keys, preferred_element_type=F32)
            if m is not None:
                psum = l * alpha + psum
                o = acc[at, :] * alpha + o
            acc[at, :] = o
            return top, psum

        def attend(who, first, count):
            m, l = state.get(who, (None, None))
            state[who] = attend_rows(who * slab, slab, m, l, first, count)

        def finished(base, n, m, l):
            mean_key = acc[base : base + n, :] / l
            return (mean_key * scale1 + base1).astype(BF16), m + jnp.log(l) * LOG2E

        diag = lax.broadcasted_iota(jnp.int32, (slab, width), 0) == lax.broadcasted_iota(
            jnp.int32, (slab, width), 1
        )

        OWN, OTHER = 0, 1
        make_queries(own, 0)
        pass_on(6, 7)
        to_partner.wait_recv()
        make_queries(xq[...].astype(F32), slab)
        pass_on(7, 8)
        start(sibs[3:5])
        mates(0)
        attend(OTHER, 0, 1)
        mates(1)
        attend(OTHER, 1, 2)
        pass_on(8, 9)
        mates(2)
        attend(OTHER, 3, 2)
        pass_on(9, 10)
        attend(OWN, 0, 1)
        pass_on(10, 11)
        attend(OWN, 1, 2)
        pass_on(11, 12)
        start(sibs[5:7])
        attend(OWN, 3, 2)
        pass_on(12, 13)
        mates(3)
        attend(OTHER, 5, 2)
        pass_on(13, 14)
        sibs[7].start()
        mates(4)
        halfway = slab // 2
        halves = [slice(0, halfway), slice(halfway, slab)]
        part_copies = [
            send(part.at[pl.ds(i * halfway, halfway)], partin.at[pl.ds(i * halfway, halfway)], tail_s, misc_r.at[1 + i], partner)
            for i in range(2)
        ]
        lse_copy = send(lse, lsein, lse_s, misc_r.at[3], partner)
        m, l = state[OTHER]
        weights = []
        for i, at in enumerate(halves):
            top, total_l = attend_rows(slab + i * halfway, halfway, m[at], l[at], 7, 1)
            part[at, :], w = finished(slab + i * halfway, halfway, top, total_l)
            weights.append(w)
            if i == 1:
                w = jnp.concatenate(weights, axis=0)
                lse[...] = jnp.sum(jnp.where(diag, w, 0.0), axis=0, keepdims=True)
                lse_copy.start()
            part_copies[i].start()
        attend(OWN, 5, 2)
        attend(OWN, 7, 1)
        o1, w1 = finished(0, slab, *state[OWN])
        y1 = jnp.dot(o1, w4[2], preferred_element_type=F32)
        base = kv[0, 0:slab].astype(F32) + vrow(2)
        lse_copy.wait_recv()
        w2 = jnp.sum(jnp.where(diag, lsein[...], 0.0), axis=1, keepdims=True)
        top = jnp.maximum(w1, w2)
        e1 = jnp.exp2(w1 - top)
        e2 = jnp.exp2(w2 - top)
        inv = 1.0 / (e1 + e2)
        base = base + y1 * (e1 * inv)
        e2 = e2 * inv
        mixed = []
        for i, at in enumerate(halves):
            part_copies[i].wait_recv()
            y2 = jnp.dot(partin[at, :], w4[2], preferred_element_type=F32)
            mixed.append((base[at] + y2 * e2[at]).astype(BF16))
        mixed = jnp.concatenate(mixed, axis=0)
        curm[0:slab, :] = mixed
        top_row = pl.ds(0, cols)
        low_row = pl.ds(slab, cols)
        bottom_row = pl.ds(cols, slab - cols)
        halos = [
            send(curm.at[top_row], earm.at[top_row], tail_s, misc_r.at[4], (later, h)),
            send(curm.at[bottom_row], earm.at[bottom_row], tail_s, misc_r.at[5], (later, h)),
            send(curm.at[top_row], curm.at[low_row], tail_s, misc_r.at[6], (f, above)),
            send(earm.at[top_row], earm.at[low_row], tail_s, misc_r.at[7], (f, above)),
        ]
        local_stats(mixed.astype(F32), 2)
        start(far2)
        start(halos[:2])
        told(2)
        merge_to(2, 3)
        start(near2)
        halos[2].start()
        halos[0].wait_recv()
        halos[3].start()
        told(3)
        mean2, rstd2 = group_stats(3)
        scale2 = vrow(3) * rstd2
        shift2 = vrow(4)

        last_col = lax.broadcasted_iota(jnp.int32, (cols, width), 0) == cols - 1

        def activate(src, which, r, keep):
            x = src[r * cols : (r + 1) * cols, :].astype(F32)
            v = (x - mean2) * scale2 + shift2
            y = v / (1.0 + jnp.exp(-v))
            if keep is not None:
                y = jnp.where(keep, y, 0.0)
            act[which, 0, r * cols : (r + 1) * cols, :] = y.astype(BF16)
            y = jnp.where(last_col, 0.0, pltpu.roll(y, cols - 1, 0))
            act[which, 1, r * cols : (r + 1) * cols, :] = y.astype(BF16)

        has_below = h < nh - 1
        has_sooner = f > 0
        for r in range(rows):
            activate(curm, 0, r, None)
        for copy in halos[1:]:
            copy.wait_recv()
        activate(curm, 0, rows, has_below)
        for r in range(rows):
            activate(earm, 1, r, has_sooner)
        activate(earm, 1, rows, jnp.logical_and(has_below, has_sooner))
        up_copy.wait()

        taps = (((0, 1),), ((0, 2), (1, 0)))
        for b in range(2):
            for c in range(2):
                wins = [(rs, cs, q, r) for rs, q in taps[b] for cs, r in taps[c]]

                def windows(which):
                    parts = [act[which, cs, rs * cols : rs * cols + slab, :] for rs, cs, _, _ in wins]
                    return parts[0] if len(parts) == 1 else jnp.concatenate(parts, axis=1)

                def weights(p):
                    parts = [wupv[p, q, r] for _, _, q, r in wins]
                    return parts[0] if len(parts) == 1 else jnp.concatenate(parts, axis=0)

                current = windows(0)
                both = jnp.dot(
                    current,
                    jnp.concatenate([weights(0), weights(1)], axis=1),
                    preferred_element_type=F32,
                )
                y0 = both[:, 0:width] + jnp.dot(windows(1), weights(2), preferred_element_type=F32)
                for a, y in ((0, y0), (1, both[:, width:])):
                    y = y + vrow(5)
                    for i in range(rows):
                        for n in range(lanes):
                            stage[a, i, n, pl.ds(c, cols, stride=2), :] = y[
                                i * cols : (i + 1) * cols, n * 128 : (n + 1) * 128
                            ]
            for a in range(2):
                for i in range(rows):
                    for n in range(lanes):
                        out[a, 2 * i + b, :, n * 128 : (n + 1) * 128] = stage[a, i, n].astype(BF16)

        took(kv_s, kv)
        took(tail_s, act.at[0])
        lse_copy.wait_send()
        for slot in range(4):
            took(st_s.at[slot], st.at[slot, pl.ds(1, group - 1)])

    slab2 = 2 * slab
    dma = pltpu.SemaphoreType.DMA
    scratch = [
        pltpu.VMEM((NSLOT, slab2, width), BF16),
        pltpu.VMEM((slab, width), BF16),
        pltpu.VMEM((slab2, width), BF16),
        pltpu.VMEM((slab2, width), F32),
        pltpu.VMEM((slab, width), BF16),
        pltpu.VMEM((slab, width), BF16),
        pltpu.VMEM((1, width), F32),
        pltpu.VMEM((1, width), F32),
        pltpu.VMEM((4, width, width), BF16),
        pltpu.VMEM((3, 3, 3, width, width), BF16),
        *[pltpu.VMEM((width,), F32)] * 6,
        pltpu.VMEM((width, width), BF16),
        pltpu.VMEM((width, 128), BF16),
        pltpu.VMEM((4, group, 1, 256), F32),
        pltpu.VMEM((slab + cols, width), BF16),
        pltpu.VMEM((slab + cols, width), BF16),
        pltpu.VMEM((2, 2, slab + cols, width), BF16),
        pltpu.VMEM((2, rows, lanes, 2 * cols, 128), F32),
        dma((4,)),
        dma((4,)),
        dma,
        dma((steps,)),
        dma((5,)),
        dma,
        dma((8,)),
        dma,
        dma((3,)),
        dma((6,)),
    ]
    return kernel, scratch


def solution(mesh):
    nf, nh = mesh.shape["frames"], mesh.shape["height"]

    def local(
        latent, first_gain, first_shift, query_weight, key_weight, value_weight, out_weight, out_bias,
        second_gain, second_shift, up_weight, up_bias,
    ):
        _, rows, cols, width = latent.shape
        kernel, scratch = make_kernel(nf, nh, rows, cols, width)

        out = pl.pallas_call(
            kernel,
            out_shape=pltpu.VMEM((2, 2 * rows, 2 * cols, width), BF16),
            in_specs=[pl.BlockSpec(memory_space=pl.ANY)] * 12,
            out_specs=pl.BlockSpec(memory_space=pltpu.VMEM),
            scratch_shapes=scratch,
            compiler_params=pltpu.CompilerParams(
                collective_id=0, has_side_effects=True, vmem_limit_bytes=56 * 1024 * 1024
            ),
            name="decoder_window",
        )(
            latent.reshape(rows * cols, width),
            first_gain, first_shift,
            query_weight, key_weight, value_weight, out_weight,
            out_bias, second_gain, second_shift,
            up_weight, up_bias,
        )
        return out

    whole = P("frames", "height", None, None)
    return jax.shard_map(
        local, mesh=mesh, in_specs=(whole,) + (P(),) * 11, out_specs=whole, check_vma=False
    )
```
